32 devices in a mesh: ctx: 4 (over y, x), wsh: 8 (over z, core).
Axes of the slice: x: 2, y: 2, z: 4, core: 2. Of those that a mesh axis runs over, the one named last changes fastest.
Arguments:
- tokens: bfloat16 [8, 2048, 768], P('wsh', 'ctx'), may hold values from -6 to 6
- cluster_order: int32 [8, 2048], P('wsh', 'ctx'), may hold values from 0 to 2047, as said below
- qkv_weight: bfloat16 [768, 2304], P('wsh'), may hold values from -0.21875 to 0.21875
- query_bias: bfloat16 [768], P('wsh'), may hold values from -3 to 3
- value_bias: bfloat16 [768], P('wsh'), may hold values from -1.25 to 1.25
- out_weight: bfloat16 [768, 768], P('wsh'), may hold values from -1.25 to 1.25
- out_bias: bfloat16 [768], P('wsh'), may hold values from -1.75 to 1.75
- first_gain: bfloat16 [768], P('wsh'), may hold values from 0.25 to 1.75
- first_shift: bfloat16 [768], P('wsh'), may hold values from -1.75 to 1.75
- up_weight: bfloat16 [768, 3072], P('wsh'), may hold values from -0.21875 to 0.21875
- up_bias: bfloat16 [3072], P('wsh'), may hold values from -3 to 3
- down_weight: bfloat16 [3072, 768], P('wsh'), may hold values from -0.109375 to 0.109375
- down_bias: bfloat16 [768], P('wsh'), may hold values from -1.75 to 1.75
- second_gain: bfloat16 [768], P('wsh'), may hold values from 0.25 to 1.75
- second_shift: bfloat16 [768], P('wsh'), may hold values from -1.75 to 1.75
- cotangent: bfloat16 [8, 2048, 768], P('wsh', 'ctx'), may hold values from -6 to 6
Outputs:
- layer_out: bfloat16 [8, 2048, 768], P('wsh', 'ctx')
- grad_tokens: float32 [8, 2048, 768], P('wsh', 'ctx')
- grad_qkv_weight: float32 [768, 2304], P('wsh')
- grad_query_bias: float32 [768], P('wsh')
- grad_value_bias: float32 [768], P('wsh')
- grad_out_weight: float32 [768, 768], P('wsh')
- grad_out_bias: float32 [768], P('wsh')
- grad_first_gain: float32 [768], P('wsh')
- grad_first_shift: float32 [768], P('wsh')
- grad_up_weight: float32 [768, 3072], P('wsh')
- grad_up_bias: float32 [3072], P('wsh')
- grad_down_weight: float32 [3072, 768], P('wsh')
- grad_down_bias: float32 [768], P('wsh')
- grad_second_gain: float32 [768], P('wsh')
- grad_second_shift: float32 [768], P('wsh')
The draws below stay inside these ranges and needn't reach their ends.
Inputs may be any that keep to these rules, and one draw needn't show every extreme that they name: `cluster_order`: each stream's row is a permutation of its positions. The stream is cut into four documents, each a multiple of 128 tokens long, the longest exactly 1024; the permutation maps every document's positions onto themselves, so each cluster lies within one document.
All inputs are finite; a program needn't handle non-finite values.
Results may differ from the reference program's by a relative error of at most 0.02.
Values may be sent and summed in bfloat16 or wider, within the bound.
A program may use at most 128 MiB of HBM per device.

```python
import jax
import jax.numpy as jnp
from jax import lax

D = 768
HEAD_DIM = 64
FF = 3072
CLUSTER = 128
GROUP_TOK = 2048
GROUPS = 8


def one_order(key):
    blocks = GROUP_TOK // CLUSTER
    longest = blocks // 2
    remain = blocks - longest
    first_key, second_key, third_key = jax.random.split(key, 3)
    cut_points = jnp.sort(jax.random.permutation(first_key, remain - 1)[:2].astype(jnp.int32) + 1)
    pieces = jnp.stack([jnp.array(longest, jnp.int32), cut_points[0], cut_points[1] - cut_points[0], jnp.array(remain, jnp.int32) - cut_points[1]]).astype(jnp.int32)
    pieces = pieces[jax.random.permutation(second_key, 4)]
    starts = ((jnp.cumsum(pieces) - pieces) * CLUSTER).astype(jnp.int32)
    places = jnp.arange(GROUP_TOK, dtype=jnp.int32)
    document = jnp.sum((places[:, None] >= starts[None, :]).astype(jnp.int32), axis=1) - 1
    scores = document * GROUP_TOK + jax.random.permutation(third_key, GROUP_TOK).astype(jnp.int32)
    return jnp.argsort(scores, stable=True).astype(jnp.int32)


def draw_cluster_order(key, part):
    stream_keys = jax.random.split(jax.random.fold_in(key, 17), GROUPS)
    return jax.vmap(one_order)(stream_keys)


def shard_levels(own_key, extent, cuts, smallest, high):
    loudness, own = 1.0, jax.random.fold_in(own_key, 6)
    for position, shards_of in cuts:
        steps = jnp.exp(jax.random.uniform(jax.random.fold_in(own, position), (shards_of,), jnp.float32, smallest / len(cuts), high / len(cuts)))
        loudness = loudness * jnp.repeat(steps, extent[position] // shards_of).reshape([-1 if axis == position else 1 for axis in range(len(extent))])
    return loudness


def bell_draw(rng, shape, deviation, most, cuts=(), kind=jnp.bfloat16):
    level = shard_levels(rng, shape, cuts, -0.22, 0.18) if cuts else 1.0
    values = jax.random.normal(rng, shape, jnp.float32) * deviation * level
    return jnp.minimum(jnp.maximum(values, -most), most).astype(kind)


def setup_inputs(seed: int = 0) -> dict:
    key_of = jax.random.split(jax.random.key(seed), 17)
    tokens = bell_draw(key_of[0], (GROUPS, GROUP_TOK, D), 1.0, 6.0, ((0, 8), (1, 4)))
    cluster_order = draw_cluster_order(jax.random.fold_in(key_of[16], 71), 0)
    qkv_weight = bell_draw(key_of[2], (D, 3 * D), D ** -0.5, 0.21875, ((0, 8),))
    query_bias = bell_draw(key_of[3], (D,), 0.5, 3.0, ((0, 8),))
    value_bias = bell_draw(key_of[4], (D,), 0.2, 1.25, ((0, 8),))
    out_weight = bell_draw(key_of[5], (D, D), (D // 32) ** -0.5, 1.25, ((0, 8),))
    out_bias = bell_draw(key_of[6], (D,), 0.3, 1.75, ((0, 8),))
    first_gain = jnp.clip(1.0 + 0.15 * jax.random.normal(key_of[7], (D,), jnp.float32), 0.25, 1.75).astype(jnp.bfloat16)
    first_shift = bell_draw(key_of[8], (D,), 0.3, 1.75, ((0, 8),))
    up_weight = bell_draw(key_of[9], (D, FF), D ** -0.5, 0.21875, ((0, 8),))
    up_bias = bell_draw(key_of[10], (FF,), 0.5, 3.0, ((0, 8),))
    down_weight = bell_draw(key_of[11], (FF, D), FF ** -0.5, 0.109375, ((0, 8),))
    down_bias = bell_draw(key_of[12], (D,), 0.3, 1.75, ((0, 8),))
    second_gain = jnp.clip(1.0 + 0.15 * jax.random.normal(key_of[13], (D,), jnp.float32), 0.25, 1.75).astype(jnp.bfloat16)
    second_shift = bell_draw(key_of[14], (D,), 0.3, 1.75, ((0, 8),))
    cotangent = bell_draw(key_of[15], (GROUPS, GROUP_TOK, D), 1.0, 6.0, ((0, 8), (1, 4)))
    return {"tokens": tokens, "cluster_order": cluster_order, "qkv_weight": qkv_weight, "query_bias": query_bias, "value_bias": value_bias, "out_weight": out_weight, "out_bias": out_bias, "first_gain": first_gain, "first_shift": first_shift, "up_weight": up_weight, "up_bias": up_bias, "down_weight": down_weight, "down_bias": down_bias, "second_gain": second_gain, "second_shift": second_shift, "cotangent": cotangent}


@jax.custom_vjp
def low(v):
    return lax.optimization_barrier(v.astype(jnp.bfloat16)).astype(jnp.float32)

@jax.custom_vjp
def low_back(v):
    return v

def low_keep(v):
    return (low(v), None)

def low_pass(kept, grad):
    return (grad,)

def back_keep(v):
    return (v, None)

def back_low(kept, grad):
    return (low(grad),)
low.defvjp(low_keep, low_pass)
low_back.defvjp(back_keep, back_low)
epsilon = 1e-05
highest = lax.Precision.HIGHEST

def matmul(left, right):
    return jnp.dot(left, right, precision=highest, preferred_element_type=jnp.float32)

def layer_norm(values, gain, shift):
    centre = values - lax.optimization_barrier(jnp.mean(values, axis=1, keepdims=True))
    factor = lax.rsqrt(lax.optimization_barrier(jnp.mean(centre * centre, axis=1, keepdims=True)) + epsilon)
    return centre * factor * gain + shift

def stream_forward(inputs, order, params):
    qkv_w, q_shift, v_shift, o_weight, o_shift, gain_one, shift_one, u_weight, u_shift, d_weight, d_shift, gain_two, shift_two = params
    width = inputs.shape[1]
    heads = width // HEAD_DIM
    blocks = inputs.shape[0] // CLUSTER
    bias_all = jnp.concatenate([q_shift, jnp.zeros_like(q_shift), v_shift])
    projected = low(low_back(matmul(inputs, qkv_w) + bias_all))
    picked = projected[order]
    query = picked[:, :width].reshape(blocks, CLUSTER, heads, HEAD_DIM)
    keyed = picked[:, width:2 * width].reshape(blocks, CLUSTER, heads, HEAD_DIM)
    valued = picked[:, 2 * width:].reshape(blocks, CLUSTER, heads, HEAD_DIM)
    scores = low_back(jnp.einsum('cihd,cjhd->chij', query, keyed, precision=highest) * HEAD_DIM ** (-0.5))
    places = order.reshape(blocks, CLUSTER)
    visible = (places[:, None, :] <= places[:, :, None])[:, None, :, :]
    masked = jnp.where(visible, scores, -1e+30)
    row_max = lax.optimization_barrier(jnp.max(masked, axis=3, keepdims=True))
    expd = jnp.where(visible, jnp.exp(masked - row_max), 0.0)
    probs = low(expd / lax.optimization_barrier(jnp.sum(expd, axis=3, keepdims=True)))
    context = jnp.einsum('chij,cjhd->cihd', probs, valued, precision=highest).reshape(inputs.shape[0], width)
    context = low(low_back(context))
    branch = low(low_back(matmul(context, o_weight) + o_shift))
    attended = jnp.zeros_like(inputs).at[order].set(branch)
    first_out = layer_norm(inputs + attended, gain_one, shift_one)
    pre_act = low_back(matmul(low(first_out), u_weight) + u_shift)
    hidden = low(jax.nn.gelu(pre_act, approximate=False))
    second_in = first_out + low_back(matmul(hidden, d_weight) + d_shift)
    return layer_norm(second_in, gain_two, shift_two)

def widen(value):
    return value.astype(jnp.float32)

def reference(tokens, cluster_order, qkv_weight, query_bias, value_bias, out_weight, out_bias, first_gain, first_shift, up_weight, up_bias, down_weight, down_bias, second_gain, second_shift, cotangent):
    params = jax.tree.map(widen, (qkv_weight, query_bias, value_bias, out_weight, out_bias, first_gain, first_shift, up_weight, up_bias, down_weight, down_bias, second_gain, second_shift))

    def one_stream(carry, stream):
        inputs, order, grad_top = stream

        def forward_here(rows_in, weights):
            return stream_forward(rows_in, order, weights)
        result, pullback = jax.vjp(forward_here, inputs, params)
        grad_in, grad_params = pullback(grad_top)
        carry = jax.tree.map(jnp.add, carry, grad_params)
        return (carry, (result.astype(jnp.bfloat16), grad_in))
    initial = jax.tree.map(jnp.zeros_like, params)
    totals, stacked = lax.scan(one_stream, initial, (tokens.astype(jnp.float32), cluster_order, cotangent.astype(jnp.float32)))
    return (stacked[0], stacked[1], totals[0], totals[1], totals[2], totals[3], totals[4], totals[5], totals[6], totals[7], totals[8], totals[9], totals[10], totals[11], totals[12])
```

```python
import jax
import jax.numpy as jnp
from jax import lax
from jax.sharding import PartitionSpec as P

HEAD_DIM = 64
CLUSTER = 128


epsilon = 1e-05


def inner(left, right):
    return lax.dot_general(
        left, right, (((0,), (0,)), ((), ())), preferred_element_type=jnp.float32
    )


def times_transposed(left, right):
    return lax.dot_general(
        left, right, (((1,), (1,)), ((), ())), preferred_element_type=jnp.float32
    )


def normalize(values):
    centre = values - jnp.mean(values, axis=1, keepdims=True)
    factor = lax.rsqrt(jnp.mean(centre * centre, axis=1, keepdims=True) + epsilon)
    return (centre * factor, factor)


def norm_back(grad_out, normed, factor, gain):
    grad_normed = grad_out * gain
    return factor * (
        grad_normed
        - jnp.mean(grad_normed, axis=1, keepdims=True)
        - normed * jnp.mean(grad_normed * normed, axis=1, keepdims=True)
    )


def on_device(
    tokens,
    cluster_order,
    qkv_weight,
    query_bias,
    value_bias,
    out_weight,
    out_bias,
    first_gain,
    first_shift,
    up_weight,
    up_bias,
    down_weight,
    down_bias,
    second_gain,
    second_shift,
    cotangent,
):
    order = cluster_order[0]
    rows = tokens.shape[1]
    width = tokens.shape[2]
    heads = width // HEAD_DIM
    blocks = rows // CLUSTER
    group_rows = rows * lax.axis_size("ctx")
    first_row = lax.axis_index("ctx") * rows
    factor_qk = HEAD_DIM ** (-0.5)
    small = [
        query_bias,
        value_bias,
        out_bias,
        first_gain,
        first_shift,
        down_bias,
        second_gain,
        second_shift,
        up_bias,
    ]
    sizes = [v.shape[0] for v in small]
    packed = lax.all_gather(jnp.concatenate(small), "wsh", axis=0, tiled=False)
    spots = [sum(sizes[:i]) for i in range(len(sizes))]
    (qbias, vbias, obias, gain_one, shift_one, dbias, gain_two, shift_two, ubias) = [
        packed[:, s : s + n].reshape(-1).astype(jnp.float32) for s, n in zip(spots, sizes)
    ]
    whole_order = lax.all_gather(order, "ctx", axis=0, tiled=True)
    both = lax.all_gather(
        jnp.concatenate([tokens[0], cotangent[0]], axis=1), "ctx", axis=0, tiled=True
    )
    whole_qkv = lax.all_gather(qkv_weight, "wsh", axis=0, tiled=True)
    whole_out = lax.all_gather(out_weight, "wsh", axis=0, tiled=True)
    whole_up = lax.all_gather(up_weight, "wsh", axis=0, tiled=True)
    whole_down = lax.all_gather(down_weight, "wsh", axis=0, tiled=True)
    take = (order[:, None] == jnp.arange(group_rows, dtype=jnp.int32)[None, :]).astype(jnp.bfloat16)
    home = (
        (first_row + jnp.arange(rows, dtype=jnp.int32))[:, None] == whole_order[None, :]
    ).astype(jnp.bfloat16)
    mine = jnp.dot(take, both, preferred_element_type=jnp.float32)
    inputs = mine[:, :width].astype(jnp.bfloat16)
    grad_top = mine[:, width:]
    qkv_shift = jnp.concatenate([qbias, jnp.zeros((width,), jnp.float32), vbias])
    own_qkv = (jnp.dot(inputs, whole_qkv, preferred_element_type=jnp.float32) + qkv_shift).astype(
        jnp.bfloat16
    )
    query = own_qkv[:, :width].reshape(blocks, CLUSTER, heads, HEAD_DIM)
    keyed = own_qkv[:, width : 2 * width].reshape(blocks, CLUSTER, heads, HEAD_DIM)
    valued = own_qkv[:, 2 * width :].reshape(blocks, CLUSTER, heads, HEAD_DIM)
    places = order.reshape(blocks, CLUSTER)
    visible = (places[:, None, :] <= places[:, :, None])[:, None, :, :]
    scores = (
        jnp.einsum("cihd,cjhd->chij", query, keyed, preferred_element_type=jnp.float32) * factor_qk
    )
    masked = jnp.where(visible, scores, -1e30)
    row_max = jnp.max(masked, axis=3, keepdims=True)
    expd = jnp.where(visible, jnp.exp(masked - row_max), 0.0)
    total = jnp.sum(expd, axis=3, keepdims=True)
    probs_full = expd / total
    probs = probs_full.astype(jnp.bfloat16)
    context = (
        jnp.einsum("chij,cjhd->cihd", probs, valued, preferred_element_type=jnp.float32)
        .astype(jnp.bfloat16)
        .reshape(rows, width)
    )
    attended = (
        (jnp.dot(context, whole_out, preferred_element_type=jnp.float32) + obias)
        .astype(jnp.bfloat16)
        .astype(jnp.float32)
    )
    resid = inputs.astype(jnp.float32) + attended
    first_norm, first_factor = normalize(resid)
    first_out = first_norm * gain_one + shift_one
    first_low = first_out.astype(jnp.bfloat16)
    pre_act = jnp.dot(first_low, whole_up, preferred_element_type=jnp.float32) + ubias
    half = 0.5 * (1.0 + lax.erf(pre_act * 0.7071067811865476))
    hidden = (pre_act * half).astype(jnp.bfloat16)
    slope = half + pre_act * jnp.exp(-0.5 * pre_act * pre_act) * 0.3989422804014327
    second_in = first_out + jnp.dot(hidden, whole_down, preferred_element_type=jnp.float32) + dbias
    second_norm, second_factor = normalize(second_in)
    layer_out = (second_norm * gain_two + shift_two).astype(jnp.bfloat16)
    group_out = lax.all_gather(layer_out, "ctx", axis=0, tiled=True)
    out_home = jnp.dot(home, group_out, preferred_element_type=jnp.float32).astype(jnp.bfloat16)
    grad_gain_two = jnp.sum(grad_top * second_norm, axis=0)
    grad_shift_two = jnp.sum(grad_top, axis=0)
    grad_second = norm_back(grad_top, second_norm, second_factor, gain_two)
    grad_branch2 = grad_second.astype(jnp.bfloat16)
    grad_down_w = inner(hidden, grad_branch2).astype(jnp.bfloat16)
    grad_down_b = jnp.sum(grad_branch2.astype(jnp.float32), axis=0)
    grad_hidden = times_transposed(grad_branch2, whole_down)
    grad_pre = (grad_hidden * slope).astype(jnp.bfloat16)
    grad_up_w = inner(first_low, grad_pre).astype(jnp.bfloat16)
    grad_up_b = jnp.sum(grad_pre.astype(jnp.float32), axis=0)
    grad_first = grad_second + times_transposed(grad_pre, whole_up)
    grad_gain_one = jnp.sum(grad_first * first_norm, axis=0)
    grad_shift_one = jnp.sum(grad_first, axis=0)
    grad_resid = norm_back(grad_first, first_norm, first_factor, gain_one)
    grad_attended = grad_resid.astype(jnp.bfloat16)
    grad_out_b = jnp.sum(grad_attended.astype(jnp.float32), axis=0)
    grad_out_w = inner(context, grad_attended).astype(jnp.bfloat16)
    grad_context = (
        times_transposed(grad_attended, whole_out)
        .astype(jnp.bfloat16)
        .reshape(blocks, CLUSTER, heads, HEAD_DIM)
    )
    grad_probs = jnp.einsum(
        "cihd,cjhd->chij", grad_context, valued, preferred_element_type=jnp.float32
    )
    grad_valued = jnp.einsum(
        "chij,cihd->cjhd", probs, grad_context, preferred_element_type=jnp.float32
    ).astype(jnp.bfloat16)
    inner_sum = jnp.sum(probs_full * grad_probs, axis=3, keepdims=True)
    grad_scores = (probs_full * (grad_probs - inner_sum)).astype(jnp.bfloat16)
    grad_query = (
        jnp.einsum("chij,cjhd->cihd", grad_scores, keyed, preferred_element_type=jnp.float32)
        * factor_qk
    ).astype(jnp.bfloat16)
    grad_keyed = (
        jnp.einsum("chij,cihd->cjhd", grad_scores, query, preferred_element_type=jnp.float32)
        * factor_qk
    ).astype(jnp.bfloat16)
    own_grad = jnp.concatenate(
        [
            grad_query.reshape(rows, width),
            grad_keyed.reshape(rows, width),
            grad_valued.reshape(rows, width),
        ],
        axis=1,
    )
    grad_query_b = jnp.sum(own_grad[:, :width].astype(jnp.float32), axis=0)
    grad_value_b = jnp.sum(own_grad[:, 2 * width :].astype(jnp.float32), axis=0)
    grad_qkv_w = inner(inputs, own_grad).astype(jnp.bfloat16)
    grad_inputs = (grad_resid + times_transposed(own_grad, whole_qkv)).astype(jnp.bfloat16)
    group_in = lax.all_gather(grad_inputs, "ctx", axis=0, tiled=True)
    in_home = jnp.dot(home, group_in, preferred_element_type=jnp.float32)

    def summed(grad):
        part = lax.psum_scatter(grad, "wsh", scatter_dimension=0, tiled=True)
        return lax.psum(part, "ctx").astype(jnp.float32)

    sums = [summed(g) for g in (grad_down_w, grad_up_w, grad_out_w, grad_qkv_w)]
    small_grads = [
        grad_query_b,
        grad_value_b,
        grad_out_b,
        grad_gain_one,
        grad_shift_one,
        grad_down_b,
        grad_gain_two,
        grad_shift_two,
        grad_up_b,
    ]
    parts = lax.axis_size("wsh")
    table = jnp.concatenate([g.reshape(parts, -1) for g in small_grads], axis=1)
    table = lax.psum(table, ("ctx", "wsh"))
    own = lax.dynamic_slice_in_dim(table, lax.axis_index("wsh"), 1, 0)[0]
    (g_q, g_v, g_o, g_g1, g_s1, g_d, g_g2, g_s2, g_u) = [
        own[s : s + n] for s, n in zip(spots, sizes)
    ]
    return (
        out_home[None],
        in_home[None],
        sums[3],
        g_q,
        g_v,
        sums[2],
        g_o,
        g_g1,
        g_s1,
        sums[1],
        g_u,
        sums[0],
        g_d,
        g_g2,
        g_s2,
    )


def solution(mesh):
    row = P("wsh", None)
    vec = P("wsh")
    seq = P("wsh", "ctx", None)
    in_specs = (
        seq,
        P("wsh", "ctx"),
        row,
        vec,
        vec,
        row,
        vec,
        vec,
        vec,
        row,
        vec,
        row,
        vec,
        vec,
        vec,
        seq,
    )
    out_specs = (
        seq,
        seq,
        row,
        vec,
        vec,
        row,
        vec,
        vec,
        vec,
        row,
        vec,
        row,
        vec,
        vec,
        vec,
    )
    return jax.shard_map(
        on_device, mesh=mesh, in_specs=in_specs, out_specs=out_specs, check_vma=False
    )
```

```python
import functools

import jax
import jax.numpy as jnp
from jax import lax
from jax.experimental import pallas as pl
from jax.experimental.pallas import tpu as pltpu
from jax.sharding import PartitionSpec as P

HEAD_DIM = 64
CLUSTER = 128
LANES = 128
STEP = 256

epsilon = 1e-05
bf16 = jnp.bfloat16
f32 = jnp.float32


def mm(left, right):
    return lax.dot_general(left, right, (((1,), (0,)), ((), ())), preferred_element_type=f32)


def mm_nt(left, right):
    return lax.dot_general(left, right, (((1,), (1,)), ((), ())), preferred_element_type=f32)


def mm_tn(left, right):
    return lax.dot_general(left, right, (((0,), (0,)), ((), ())), preferred_element_type=f32)


def flip(index, offset):
    bit = 1
    result = index
    while bit <= offset:
        if offset & bit:
            result = result + bit * (1 - 2 * ((index // bit) % 2))
        bit *= 2
    return result


def bits_of(size):
    found, bit = [], 1
    while bit < size:
        found.append(bit)
        bit *= 2
    return found


def low_bit(value):
    return value & -value


class Flight:
    def __init__(self, copy):
        self.copy, self.leaving = copy, True
        copy.start()

    def wait_recv(self):
        self.copy.wait_recv()

    def wait_send(self):
        if self.leaving:
            self.copy.wait_send()
        self.leaving = False


class Links:
    def __init__(self, send_sem, recv_sem):
        self.send_sem, self.recv_sem, self.used = send_sem, recv_sem, 0
        self.sent = []

    def send(self, src, dst, ctx, wsh):
        n = self.used
        self.used += 1
        flight = Flight(
            pltpu.make_async_remote_copy(
                src_ref=src,
                dst_ref=dst,
                send_sem=self.send_sem.at[n],
                recv_sem=self.recv_sem.at[n],
                device_id=(ctx, wsh),
                device_id_type=pl.DeviceIdType.MESH,
            )
        )
        self.sent.append(flight)
        return flight

    def local(self, src, dst):
        n = self.used
        self.used += 1
        copy = pltpu.make_async_copy(src, dst, self.send_sem.at[n])
        copy.start()
        return copy

    def drain(self):
        for copy in self.sent:
            copy.wait_send()
        self.sent = []


class CtxGather:
    def __init__(self, links, own, buffer, ctx, wsh, count, halves):
        self.links, self.own, self.buffer, self.ctx, self.wsh = links, own, buffer, ctx, wsh
        rows = buffer.shape[1] // halves
        self.spans = [pl.ds(h * rows, rows) for h in range(halves)]
        order = bits_of(count)
        self.orders = [order, order[1::-1] + order[2:]][:halves]
        self.have = [{0: None} for _ in self.spans]
        self.step = 0
        self.steps = len(order)

    def advance(self):
        for h, span in enumerate(self.spans):
            bit = self.orders[h][self.step]
            new = {}
            for offset, arrival in self.have[h].items():
                if arrival is not None:
                    arrival.wait_recv()
                    self.have[h][offset] = None
                block = flip(self.ctx, offset)
                src = self.own.at[span] if offset == 0 else self.buffer.at[block, span]
                new[offset ^ bit] = self.links.send(
                    src, self.buffer.at[block, span], flip(self.ctx, bit), self.wsh
                )
            self.have[h].update(new)
        self.step += 1

    def need(self, offset):
        for have in self.have:
            if have[offset] is not None:
                have[offset].wait_recv()
                have[offset] = None


class WeightGather:
    def __init__(self, links, shard, whole, place, sizes, pair):
        self.links, self.shard, self.whole = links, shard, whole
        self.ctx, self.z, self.core = place
        self.zs = sizes
        self.pair = pair
        self.rows, self.columns = shard.shape
        self.bits = bits_of(sizes)[::-1]

    def row_span(self, offset, core):
        first = (flip(self.z, offset) * 2 + core) * self.rows
        return pl.ds(pl.multiple_of(first, 16), self.rows)

    def column_span(self, mine):
        if self.pair is None:
            return pl.ds(0, self.columns)
        half = self.columns // 2
        side = (self.ctx // self.pair) % 2
        if not mine:
            side = 1 - side
        return pl.ds(pl.multiple_of(side * half, LANES), half)

    def wsh_of(self, offset, core):
        return flip(self.z, offset) * 2 + core

    def start(self):
        span = self.column_span(True)
        rows = self.row_span(0, self.core)
        self.from_z, self.from_pair, self.from_core = {}, {}, []
        for bit in self.bits:
            self.from_z[bit] = self.links.send(
                self.shard.at[:, span],
                self.whole.at[rows, span],
                self.ctx,
                self.wsh_of(bit, self.core),
            )
        self.from_core.append(
            self.links.send(
                self.shard, self.whole.at[rows], self.ctx, self.wsh_of(0, 1 - self.core)
            )
        )
        self.own = self.links.local(self.shard, self.whole.at[rows])

    def to_core(self, offset, span):
        part = self.whole.at[self.row_span(offset, self.core), span]
        self.from_core.append(
            self.links.send(part, part, self.ctx, self.wsh_of(0, 1 - self.core))
        )

    def take_z(self):
        span = self.column_span(True)
        for offset in sorted(range(1, self.zs), key=lambda o: (-low_bit(o), o)):
            self.from_z[offset].wait_recv()
            part = self.whole.at[self.row_span(offset, self.core), span]
            for bit in self.bits:
                if bit < low_bit(offset):
                    self.from_z[offset + bit] = self.links.send(
                        part, part, self.ctx, self.wsh_of(bit, self.core)
                    )
            if self.pair is not None:
                self.from_pair[offset] = self.links.send(
                    part, part, flip(self.ctx, self.pair), self.wsh_of(0, self.core)
                )
            self.to_core(offset, span)

    def take_pair(self):
        if self.pair is None:
            return
        span = self.column_span(False)
        for offset, arrival in self.from_pair.items():
            arrival.wait_recv()
            self.to_core(offset, span)

    def finish(self):
        self.own.wait()
        for arrival in self.from_core:
            arrival.wait_recv()


class GradScatter:
    def __init__(self, links, whole, from_core, from_z, from_ctx, place, zs, ctxs):
        self.links, self.whole = links, whole
        self.from_core, self.from_z, self.from_ctx = from_core, from_z, from_ctx
        self.ctx, self.z, self.core = place
        self.zs, self.ctxs = zs, ctxs
        self.rows = whole.shape[0] // (2 * zs)
        self.zbits, self.cbits = bits_of(zs), bits_of(ctxs)
        self.order = sorted(range(zs), key=lambda o: -(o % 2))

    def span(self, offset, core):
        first = (flip(self.z, offset) * 2 + core) * self.rows
        return pl.ds(pl.multiple_of(first, 16), self.rows)

    def send_core(self):
        self.arrive = {}
        for offset in self.order:
            self.arrive[offset] = self.links.send(
                self.whole.at[self.span(offset, 1 - self.core)],
                self.from_core.at[offset],
                self.ctx,
                self.z * 2 + 1 - self.core,
            )

    def add(self, offset, other):
        first = (flip(self.z, offset) * 2 + self.core) * self.rows
        columns = self.whole.shape[1]
        piece = 48 if columns <= 768 else 16

        def body(i, carry):
            here = pl.ds(pl.multiple_of(first + i * piece, 16), piece)
            there = pl.ds(pl.multiple_of(i * piece, 16), piece)
            self.whole[here, :] = (
                self.whole[here, :].astype(f32) + other[there, :].astype(f32)
            ).astype(bf16)
            return carry

        lax.fori_loop(0, self.rows // piece, body, 0)

    def add_core(self):
        for offset in self.order:
            self.arrive[offset].wait_recv()
            self.add(offset, self.from_core.at[offset])

    def z_slot(self, bit, offset):
        first = 0
        for earlier in self.zbits:
            if earlier == bit:
                break
            first += self.zs // (2 * earlier)
        return first + offset // (2 * bit)

    def send_z(self, bit):
        self.arrive = {}
        for offset in range(bit, self.zs, 2 * bit):
            self.arrive[offset - bit] = self.links.send(
                self.whole.at[self.span(offset, self.core)],
                self.from_z.at[self.z_slot(bit, offset - bit)],
                self.ctx,
                flip(self.z, bit) * 2 + self.core,
            )

    def add_z(self, bit):
        for offset, arrival in self.arrive.items():
            arrival.wait_recv()
            self.add(offset, self.from_z.at[self.z_slot(bit, offset)])

    def send_ctx(self, bit):
        self.arrive = self.links.send(
            self.whole.at[self.span(0, self.core)],
            self.from_ctx.at[self.cbits.index(bit)],
            flip(self.ctx, bit),
            self.z * 2 + self.core,
        )

    def add_ctx(self, bit):
        self.arrive.wait_recv()
        self.arrive.wait_send()
        self.add(0, self.from_ctx.at[self.cbits.index(bit)])

    def steps(self):
        self.add_core()
        for bit in self.zbits:
            self.send_z(bit)
            yield
            self.add_z(bit)
        for bit in self.cbits:
            self.send_ctx(bit)
            yield
            self.add_ctx(bit)
        yield


class TableSum:
    def __init__(self, links, table, slots, place, zs, ctxs):
        self.links, self.table, self.slots = links, table, slots
        self.ctx, self.z, self.core = place
        self.hops = (
            [(self.ctx, self.z * 2 + 1 - self.core)]
            + [(self.ctx, flip(self.z, b) * 2 + self.core) for b in bits_of(zs)]
            + [(flip(self.ctx, b), self.z * 2 + self.core) for b in bits_of(ctxs)]
        )

    def steps(self):
        for n, (ctx, wsh) in enumerate(self.hops):
            copy = self.links.send(self.table, self.slots.at[n], ctx, wsh)
            yield
            copy.wait_recv()
            copy.wait_send()
            self.table[...] = self.table[...] + self.slots[n]
        yield


def layer_kernel(
    ctxs,
    zs,
    pairs,
    tok,
    cot,
    order_column,
    order_row,
    vectors,
    qkv_shard,
    out_shard,
    up_shard,
    down_shard,
    home_out,
    home_grad,
    sum_qkv,
    sum_out,
    sum_up,
    sum_down,
    sum_small,
    all_tok,
    all_cot,
    all_out,
    all_grad,
    all_order,
    all_vectors,
    w_qkv,
    w_out,
    w_up,
    w_down,
    g_down,
    stage,
    acc,
    inputs,
    low,
    top,
    qkv,
    probs,
    context,
    turned,
    first_norm,
    first_factor,
    hidden,
    slope,
    grad_wide,
    grad_low,
    result_low,
    back_low,
    rows_768,
    row_up,
    small,
    small_slots,
    core_qkv,
    core_out,
    core_up,
    core_down,
    z_qkv,
    z_out,
    z_up,
    z_down,
    c_qkv,
    c_out,
    c_up,
    c_down,
    send_sem,
    recv_sem,
):
    rows, width = tok.shape
    wide = up_shard.shape[1]
    pairs_of_heads = width // LANES
    blocks = rows // CLUSTER
    scale = HEAD_DIM**-0.5
    ctx = lax.axis_index("ctx")
    wsh = lax.axis_index("wsh")
    z, core = wsh // 2, wsh % 2
    place = (ctx, z, core)
    links = Links(send_sem, recv_sem)

    barrier = pltpu.get_barrier_semaphore()
    peers = (
        [(ctx, z * 2 + 1 - core)]
        + [(ctx, flip(z, b) * 2 + core) for b in bits_of(zs)]
        + [(flip(ctx, b), wsh) for b in bits_of(ctxs)]
    )
    for peer in peers:
        pl.semaphore_signal(barrier, 1, device_id=peer, device_id_type=pl.DeviceIdType.MESH)
    pl.semaphore_wait(barrier, len(peers))

    tok_gather = CtxGather(links, tok, all_tok, ctx, wsh, ctxs, 2)
    cot_gather = CtxGather(links, cot, all_cot, ctx, wsh, ctxs, 2)
    order_gather = CtxGather(links, order_row, all_order, ctx, wsh, ctxs, 1)
    tok_gather.advance()
    order_gather.advance()
    vec_own = links.local(vectors, all_vectors.at[wsh])
    vec_first = links.send(vectors, all_vectors.at[wsh], ctx, z * 2 + 1 - core)
    gathers = [
        WeightGather(links, s, w, place, zs, p)
        for s, w, p in zip(
            (qkv_shard, out_shard, up_shard, down_shard), (w_qkv, w_out, w_up, w_down), pairs
        )
    ]
    for gather in gathers:
        gather.start()

    vec_own.wait()
    vec_first.wait_recv()
    have = 2
    for bit in bits_of(zs):
        span = pl.ds((wsh // have) * have, have)
        copy = links.send(all_vectors.at[span], all_vectors.at[span], ctx, flip(z, bit) * 2 + core)
        copy.wait_recv()
        have *= 2
    while tok_gather.step < tok_gather.steps:
        tok_gather.advance()
        order_gather.advance()

    rows_768[...] = jnp.zeros_like(rows_768)
    row_up[...] = jnp.zeros_like(row_up)
    length = width // (2 * zs)

    def spread(part, row, spot, target, target_row):
        first = min(spot // LANES * LANES, target.shape[1] - STEP)
        j = lax.broadcasted_iota(jnp.int32, (LANES, STEP), 0)
        col = lax.broadcasted_iota(jnp.int32, (LANES, STEP), 1)
        move = jnp.where((col == j + (spot - first)) & (j < length), 1.0, 0.0).astype(bf16)
        moved = mm(part, move)
        n = 8 if row is None else 1
        at = 0 if row is None else row
        where_to = pl.ds(target_row, n), pl.ds(first, STEP)
        target[where_to] = target[where_to] + moved[at : at + n]

    for s in range(2 * zs):
        part = all_vectors[s]
        spread(part, None, length * s, rows_768, 0)
        for r in range(4):
            spread(part, 8 + r, length * (4 * s + r), row_up, 0)

    def pick(gather, own, total):
        copies = {}

        def fetch(offset):
            if offset == 0:
                src = own
            else:
                gather.need(offset)
                src = gather.buffer.at[flip(ctx, offset)]
            copies[offset] = links.local(src, stage.at[offset % 2])

        fetch(0)
        for offset in range(ctxs):
            copies[offset].wait()
            if offset + 1 < ctxs:
                fetch(offset + 1)
            first = flip(ctx, offset) * rows

            def body(i, carry):
                here = pl.ds(pl.multiple_of(i * CLUSTER, CLUSTER), CLUSTER)
                place_of = order_column[here, :]
                lane = lax.broadcasted_iota(jnp.int32, (CLUSTER, LANES), 1)
                chosen = jnp.concatenate(
                    [
                        jnp.where(place_of == lane + (first + t * LANES), 1.0, 0.0).astype(bf16)
                        for t in range(rows // LANES)
                    ],
                    axis=1,
                )
                got = mm(chosen, stage[offset % 2])
                total[here, :] = got if offset == 0 else total[here, :] + got
                return carry

            lax.fori_loop(0, blocks, body, 0)

    def bring_home(gather, own, target):
        copies = {}

        def fetch(offset):
            if offset == 0:
                src = own
            else:
                gather.need(offset)
                src = gather.buffer.at[flip(ctx, offset)]
            copies[offset] = links.local(src, stage.at[offset % 2])

        fetch(0)
        for offset in range(ctxs):
            copies[offset].wait()
            if offset + 1 < ctxs:
                fetch(offset + 1)
            if offset == 0:
                places = order_row[...]
            else:
                order_gather.need(offset)
                places = all_order[flip(ctx, offset)]

            def body(i, carry):
                here = pl.ds(pl.multiple_of(i * CLUSTER, CLUSTER), CLUSTER)
                token = lax.broadcasted_iota(jnp.int32, (CLUSTER, rows), 0) + (
                    ctx * rows + i * CLUSTER
                )
                chosen = jnp.where(places[0:1, :] == token, 1.0, 0.0).astype(bf16)
                got = mm(chosen, stage[offset % 2])
                if offset > 0:
                    got = acc[here, :] + got
                if offset == ctxs - 1:
                    target[here, :] = got.astype(bf16)
                else:
                    acc[here, :] = got
                return carry

            lax.fori_loop(0, blocks, body, 0)

    def tiles(columns, body):
        def step(t, carry):
            body(t, pl.ds(pl.multiple_of(t * STEP, STEP), STEP))
            return carry

        lax.fori_loop(0, columns // STEP, step, 0)

    def row_pass(size, body):
        def step(i, carry):
            body(pl.ds(pl.multiple_of(i * size, size), size))
            return carry

        lax.fori_loop(0, rows // size, step, 0)

    def tally(vector, values):
        total = jnp.sum(values, axis=0, keepdims=True)
        for t in range(width // STEP):
            at = pl.ds(vector * (width // STEP) + t, 1)
            small[at, :] = small[at, :] + total[:, t * STEP : (t + 1) * STEP]

    small[...] = jnp.zeros_like(small)
    qbias, vbias, obias, gain1, shift1, dbias, gain2, shift2 = [
        rows_768.at[pl.ds(n, 1)] for n in range(8)
    ]

    gathers[0].take_z()
    pick(tok_gather, tok, acc)

    def keep_inputs(here):
        inputs[here, :] = acc[here, :].astype(bf16)

    row_pass(CLUSTER, keep_inputs)
    gathers[1].take_z()
    gathers[0].take_pair()
    gathers[1].take_pair()
    cot_gather.advance()
    gathers[0].finish()

    def project(t, span):
        at = pl.ds(pl.multiple_of((t % (width // STEP)) * STEP, STEP), STEP)
        part = t // (width // STEP)
        bias = jnp.where(part == 0, qbias[:, at], jnp.where(part == 2, vbias[:, at], 0.0))
        qkv[:, span] = (mm(inputs[...], w_qkv[:, span]) + bias).astype(bf16)

    tiles(3 * width, project)

    gathers[2].take_z()

    lane = lax.broadcasted_iota(jnp.int32, (1, LANES), 1)
    left = jnp.where(lane < HEAD_DIM, 1.0, 0.0).astype(bf16)
    right = jnp.where(lane < HEAD_DIM, 0.0, 1.0).astype(bf16)

    def both(values):
        return jnp.concatenate([values * left, values * right], axis=0)

    def side_by_side(values):
        return jnp.concatenate([values[:CLUSTER], values[CLUSTER:]], axis=1)

    def part_of(here, kind, pair):
        return qkv[here, kind * width + pair * LANES : kind * width + (pair + 1) * LANES]

    def attend(b, carry):
        here = pl.ds(pl.multiple_of(b * CLUSTER, CLUSTER), CLUSTER)
        visible = order_row[0:1, here] <= order_column[here, :]
        hide = jnp.where(visible, 0.0, -1e30)
        hide = jnp.concatenate([hide, hide], axis=0)
        for pair in range(pairs_of_heads):
            query, keyed, valued = [part_of(here, kind, pair) for kind in range(3)]
            scores = mm_nt(both(query), keyed) * scale + hide
            expd = jnp.exp(scores - jnp.max(scores, axis=1, keepdims=True))
            prob = expd * (1.0 / jnp.sum(expd, axis=1, keepdims=True))
            probs[b * pairs_of_heads + pair] = prob
            got = mm(side_by_side(prob.astype(bf16)), both(valued))
            context[here, pair * LANES : (pair + 1) * LANES] = got.astype(bf16)
        return carry

    lax.fori_loop(0, blocks, attend, 0)
    gathers[2].take_pair()
    gathers[3].take_z()
    while cot_gather.step < cot_gather.steps:
        cot_gather.advance()
    gathers[1].finish()

    def out_project(t, span):
        acc[:, span] = mm(context[...], w_out[:, span])

    tiles(width, out_project)

    def first_normalize(here):
        attended = (acc[here, :] + obias[...]).astype(bf16).astype(f32)
        resid = inputs[here, :].astype(f32) + attended
        centre = resid - jnp.mean(resid, axis=1, keepdims=True)
        factor = lax.rsqrt(jnp.mean(centre * centre, axis=1, keepdims=True) + epsilon)
        normed = centre * factor
        first_norm[here, :] = normed
        first_factor[here, :] = factor
        low[here, :] = (normed * gain1[...] + shift1[...]).astype(bf16)

    row_pass(64, first_normalize)
    pick(cot_gather, cot, acc)

    def keep_top(here):
        top[here, :] = acc[here, :].astype(bf16)

    row_pass(CLUSTER, keep_top)
    gathers[3].take_pair()
    gathers[2].finish()

    def feed(t, span):
        pre = mm(low[...], w_up[:, span]) + row_up[0:1, span]
        half = 0.5 * (1.0 + lax.erf(pre * 0.7071067811865476))
        hidden[:, span] = (pre * half).astype(bf16)
        slope[:, span] = (half + pre * jnp.exp(-0.5 * pre * pre) * 0.3989422804014327).astype(bf16)

    tiles(wide, feed)
    gathers[3].finish()

    def down(t, span):
        acc[:, span] = mm(hidden[...], w_down[:, span])

    tiles(width, down)

    def second_normalize(here):
        first_out = first_norm[here, :] * gain1[...] + shift1[...]
        second_in = first_out + acc[here, :] + dbias[...]
        centre = second_in - jnp.mean(second_in, axis=1, keepdims=True)
        factor = lax.rsqrt(jnp.mean(centre * centre, axis=1, keepdims=True) + epsilon)
        normed = centre * factor
        result_low[here, :] = (normed * gain2[...] + shift2[...]).astype(bf16)
        grad_top = top[here, :].astype(f32)
        tally(6, grad_top * normed)
        tally(7, grad_top)
        grad_normed = grad_top * gain2[...]
        grad = factor * (
            grad_normed
            - jnp.mean(grad_normed, axis=1, keepdims=True)
            - normed * jnp.mean(grad_normed * normed, axis=1, keepdims=True)
        )
        grad_wide[here, :] = grad
        grad = grad.astype(bf16)
        grad_low[here, :] = grad
        tally(5, grad.astype(f32))

    row_pass(64, second_normalize)

    scatters = [
        GradScatter(links, w, a, b, c, place, zs, ctxs)
        for w, a, b, c in (
            (w_qkv, core_qkv, z_qkv, c_qkv),
            (w_out, core_out, z_out, c_out),
            (w_up, core_up, z_up, c_up),
            (g_down, core_down, z_down, c_down),
        )
    ]
    out_gather = CtxGather(links, result_low, all_out, ctx, wsh, ctxs, 2)
    part_rows = wide // (2 * zs)

    def down_grad(owner):
        def body(i, carry):
            here = pl.ds(pl.multiple_of((i * 2 + owner) * part_rows, LANES // 2), part_rows)
            turned_hidden = hidden_turned(i * 2 + owner)
            g_down[here, :] = mm(turned_hidden, grad_low[...]).astype(bf16)
            return carry

        lax.fori_loop(0, zs, body, 0)

    if part_rows % LANES == 0:

        def hidden_turned(s):
            return hidden[:, pl.ds(pl.multiple_of(s * part_rows, LANES), part_rows)].T

        down_grad(1 - core)
        scatters[3].send_core()
        down_grad(core)
    else:

        def all_down(t, span):
            g_down[span, :] = mm(hidden[:, span].T, grad_low[...]).astype(bf16)

        tiles(wide, all_down)
        scatters[3].send_core()
    out_gather.advance()

    def back_hidden(t, span):
        grad = (mm_nt(grad_low[...], w_down[span, :]) * slope[:, span]).astype(bf16)
        slope[:, span] = grad
        small[pl.ds(8 * (width // STEP) + t, 1), :] = jnp.sum(
            grad.astype(f32), axis=0, keepdims=True
        )

    tiles(wide, back_hidden)
    down_steps = scatters[3].steps()
    next(down_steps)

    def back_up(t, span):
        acc[:, span] = mm_nt(slope[...], w_up[span, :])

    tiles(width, back_up)

    def first_back(here):
        grad_first = grad_wide[here, :] + acc[here, :]
        normed = first_norm[here, :]
        tally(3, grad_first * normed)
        tally(4, grad_first)
        grad_normed = grad_first * gain1[...]
        grad = first_factor[here, :] * (
            grad_normed
            - jnp.mean(grad_normed, axis=1, keepdims=True)
            - normed * jnp.mean(grad_normed * normed, axis=1, keepdims=True)
        )
        grad_wide[here, :] = grad
        grad = grad.astype(bf16)
        grad_low[here, :] = grad
        tally(2, grad.astype(f32))

    row_pass(64, first_back)
    while out_gather.step < out_gather.steps:
        out_gather.advance()
    links.drain()

    turned[...] = low[...].T

    def up_grad(t, span):
        w_up[:, span] = mm(turned[...], slope[:, span]).astype(bf16)

    tiles(wide, up_grad)
    scatters[2].send_core()

    turned[...] = context[...].T

    def back_context(t, span):
        context[:, span] = mm_nt(grad_low[...], w_out[span, :]).astype(bf16)

    tiles(width, back_context)

    def out_grad(t, span):
        w_out[:, span] = mm(turned[...], grad_low[:, span]).astype(bf16)

    tiles(width, out_grad)
    scatters[1].send_core()
    up_steps = scatters[2].steps()
    next(up_steps)
    next(down_steps)
    out_steps = scatters[1].steps()
    next(out_steps)

    def back_attend(b, carry):
        here = pl.ds(pl.multiple_of(b * CLUSTER, CLUSTER), CLUSTER)
        for pair in range(pairs_of_heads):
            query, keyed, valued = [part_of(here, kind, pair) for kind in range(3)]
            prob = probs[b * pairs_of_heads + pair]
            grad = both(context[here, pair * LANES : (pair + 1) * LANES])
            grad_prob = mm_nt(grad, valued)
            grad_valued = mm_tn(prob.astype(bf16), grad)
            inner = jnp.sum(prob * grad_prob, axis=1, keepdims=True)
            grad_score = (prob * (grad_prob - inner)).astype(bf16)
            grad_query = mm(side_by_side(grad_score), both(keyed)) * scale
            grad_keyed = mm_tn(grad_score, both(query)) * scale
            for kind, value in enumerate((grad_query, grad_keyed, grad_valued)):
                at = kind * width + pair * LANES
                qkv[here, at : at + LANES] = value.astype(bf16)
        return carry

    lax.fori_loop(0, blocks, back_attend, 0)

    def input_sums(here):
        tally(0, qkv[here, 0:width].astype(f32))
        tally(1, qkv[here, 2 * width : 3 * width].astype(f32))

    row_pass(64, input_sums)

    def back_qkv(t, span):
        back_low[:, span] = (mm_nt(qkv[...], w_qkv[span, :]) + grad_wide[:, span]).astype(bf16)

    tiles(width, back_qkv)
    grad_gather = CtxGather(links, back_low, all_grad, ctx, wsh, ctxs, 2)
    turned[...] = inputs[...].T

    def qkv_grad(t, span):
        w_qkv[:, span] = mm(turned[...], qkv[:, span]).astype(bf16)

    tiles(3 * width, qkv_grad)
    scatters[0].send_core()
    grad_gather.advance()
    table = TableSum(links, small, small_slots, place, zs, ctxs)
    table_steps = table.steps()
    next(table_steps)
    qkv_steps = scatters[0].steps()
    next(qkv_steps)
    next(table_steps)
    next(up_steps)
    next(down_steps)
    next(out_steps)
    bring_home(out_gather, result_low, home_out)
    while grad_gather.step < grad_gather.steps:
        grad_gather.advance()
    running = [down_steps, up_steps, out_steps, qkv_steps, table_steps]
    while running:
        still = []
        for steps in running:
            if next(steps, "end") != "end":
                still.append(steps)
        running = still
    bring_home(grad_gather, back_low, home_grad)
    copies = []
    for scatter, result in zip(scatters, (sum_qkv, sum_out, sum_up, sum_down)):
        copies.append(links.local(scatter.whole.at[scatter.span(0, core)], result))
    sum_small[...] = small[...]
    links.drain()
    for copy in copies:
        copy.wait()


def on_device(
    ctxs,
    wshs,
    tokens,
    cluster_order,
    qkv_weight,
    query_bias,
    value_bias,
    out_weight,
    out_bias,
    first_gain,
    first_shift,
    up_weight,
    up_bias,
    down_weight,
    down_bias,
    second_gain,
    second_shift,
    cotangent,
):
    rows, width = tokens.shape[1:]
    wide = up_weight.shape[1]
    zs = wshs // 2
    length = query_bias.shape[0]
    order = cluster_order[0]
    order_column = jnp.broadcast_to(order[:, None], (rows, LANES))
    order_row = jnp.broadcast_to(order[None, :], (8, rows))
    vectors = jnp.concatenate(
        [
            jnp.stack(
                [
                    query_bias,
                    value_bias,
                    out_bias,
                    first_gain,
                    first_shift,
                    down_bias,
                    second_gain,
                    second_shift,
                ]
            ),
            up_bias.reshape(4, length),
        ],
        axis=0,
    )
    vectors = jnp.pad(vectors, ((0, 4), (0, LANES - length)))
    small_rows = 8 * (width // STEP) + wide // STEP
    small_rows = (small_rows + 7) // 8 * 8
    heads_pairs = width // LANES
    blocks = rows // CLUSTER
    hops = 1 + len(bits_of(zs)) + len(bits_of(ctxs))
    shards = [qkv_weight.shape, out_weight.shape, up_weight.shape, down_weight.shape]
    slots = zs - 1
    sems = 4 * 2 * ctxs * 2 + 6 * zs * 4 + 4 * (4 * zs + 8) + 64

    def vmem(shape, dtype=bf16):
        return pltpu.VMEM(shape, dtype)

    anywhere = pl.BlockSpec(memory_space=pl.ANY)
    on_chip = pl.BlockSpec(memory_space=pltpu.VMEM)
    many = jax.ShapeDtypeStruct((ctxs, rows, width), bf16)
    pairs = (1, 2, 1, 2)
    results = pl.pallas_call(
        functools.partial(layer_kernel, ctxs, zs, pairs),
        out_shape=[
            jax.ShapeDtypeStruct((rows, width), bf16),
            jax.ShapeDtypeStruct((rows, width), bf16),
        ]
        + [jax.ShapeDtypeStruct(s, bf16) for s in shards]
        + [jax.ShapeDtypeStruct((small_rows, STEP), f32)]
        + [many] * 4,
        in_specs=[anywhere, anywhere, on_chip, on_chip] + [anywhere] * 5,
        out_specs=[on_chip, on_chip] + [anywhere] * 4 + [on_chip] + [anywhere] * 4,
        scratch_shapes=[
            vmem((ctxs, 8, rows), jnp.int32),
            vmem((wshs, 16, LANES)),
            vmem((width, 3 * width)),
            vmem((width, width)),
            vmem((width, wide)),
            vmem((wide, width)),
            vmem((wide, width)),
            vmem((2, rows, width)),
            vmem((rows, width), f32),
            vmem((rows, width)),
            vmem((rows, width)),
            vmem((rows, width)),
            vmem((rows, 3 * width)),
            vmem((blocks * heads_pairs, 2 * CLUSTER, CLUSTER), f32),
            vmem((rows, width)),
            vmem((width, rows)),
            vmem((rows, width), f32),
            vmem((rows, 1), f32),
            vmem((rows, wide)),
            vmem((rows, wide)),
            vmem((rows, width), f32),
            vmem((rows, width)),
            vmem((rows, width)),
            vmem((rows, width)),
            vmem((8, width), f32),
            vmem((8, wide), f32),
            vmem((small_rows, STEP), f32),
            vmem((hops, small_rows, STEP), f32),
        ]
        + [vmem((zs,) + s) for s in shards]
        + [vmem((slots,) + s) for s in shards]
        + [vmem((len(bits_of(ctxs)),) + s) for s in shards]
        + [pltpu.SemaphoreType.DMA((sems,)), pltpu.SemaphoreType.DMA((sems,))],
        compiler_params=pltpu.CompilerParams(
            collective_id=0, has_side_effects=True, vmem_limit_bytes=67043328
        ),
        name="layer",
    )(
        tokens[0],
        cotangent[0],
        order_column,
        order_row,
        vectors,
        qkv_weight,
        out_weight,
        up_weight,
        down_weight,
    )
    home_out, home_grad, sum_qkv, sum_out, sum_up, sum_down, small = results[:7]
    count = width // STEP
    whole = [small[n * count : (n + 1) * count].reshape(width) for n in range(8)]
    whole.append(small[8 * count : 8 * count + wide // STEP].reshape(wide))
    me = lax.axis_index("wsh")

    def own(vector):
        n = vector.shape[0] // wshs
        return lax.dynamic_slice_in_dim(vector, me * n, n, 0)

    (g_q, g_v, g_o, g_g1, g_s1, g_d, g_g2, g_s2, g_u) = [own(v) for v in whole]
    return (
        home_out[None],
        home_grad[None].astype(f32),
        sum_qkv.astype(f32),
        g_q,
        g_v,
        sum_out.astype(f32),
        g_o,
        g_g1,
        g_s1,
        sum_up.astype(f32),
        g_u,
        sum_down.astype(f32),
        g_d,
        g_g2,
        g_s2,
    )


def solution(mesh):
    row = P("wsh", None)
    vec = P("wsh")
    seq = P("wsh", "ctx", None)
    in_specs = (
        seq,
        P("wsh", "ctx"),
        row,
        vec,
        vec,
        row,
        vec,
        vec,
        vec,
        row,
        vec,
        row,
        vec,
        vec,
        vec,
        seq,
    )
    out_specs = (
        seq,
        seq,
        row,
        vec,
        vec,
        row,
        vec,
        vec,
        vec,
        row,
        vec,
        row,
        vec,
        vec,
        vec,
    )
    return jax.shard_map(
        functools.partial(on_device, mesh.shape["ctx"], mesh.shape["wsh"]),
        mesh=mesh,
        in_specs=in_specs,
        out_specs=out_specs,
        check_vma=False,
    )
```

```python
import functools

import jax
import jax.numpy as jnp
from jax import lax
from jax.experimental import pallas as pl
from jax.experimental.pallas import tpu as pltpu
from jax.sharding import PartitionSpec as P

HEAD_DIM = 64
CLUSTER = 128
LANES = 128
STEP = 256

epsilon = 1e-05
bf16 = jnp.bfloat16
f32 = jnp.float32


def mm(left, right):
    return lax.dot_general(left, right, (((1,), (0,)), ((), ())), preferred_element_type=f32)


def mm_nt(left, right):
    return lax.dot_general(left, right, (((1,), (1,)), ((), ())), preferred_element_type=f32)


def mm_tn(left, right):
    return lax.dot_general(left, right, (((0,), (0,)), ((), ())), preferred_element_type=f32)


def flip(index, offset):
    bit = 1
    result = index
    while bit <= offset:
        if offset & bit:
            result = result + bit * (1 - 2 * ((index // bit) % 2))
        bit *= 2
    return result


def bits_of(size):
    found, bit = [], 1
    while bit < size:
        found.append(bit)
        bit *= 2
    return found


def low_bit(value):
    return value & -value


def only_if(condition, action):
    if condition is None:
        action()
    else:
        pl.when(condition)(action)


class Flight:
    def __init__(self, copy, landing=None, sends=None, receives=None):
        self.copy, self.landing = copy, landing or copy
        self.sends, self.receives = sends, receives
        self.leaving = self.coming = True
        only_if(sends, copy.start)

    def wait_recv(self):
        if self.coming:
            only_if(self.receives, self.landing.wait_recv)
        self.coming = False

    def wait_send(self):
        if self.leaving:
            only_if(self.sends, self.copy.wait_send)
        self.leaving = False


class Links:
    def __init__(self, send_sem, recv_sem):
        self.send_sem, self.recv_sem, self.used = send_sem, recv_sem, 0
        self.sent = []

    def remote(self, n, src, dst, ctx, wsh):
        return pltpu.make_async_remote_copy(
            src_ref=src,
            dst_ref=dst,
            send_sem=self.send_sem.at[n],
            recv_sem=self.recv_sem.at[n],
            device_id=(ctx, wsh),
            device_id_type=pl.DeviceIdType.MESH,
        )

    def send(self, src, dst, ctx, wsh, landing=None, sends=None, receives=None):
        n = self.used
        self.used += 1
        if landing is not None:
            landing = self.remote(n, landing, landing, ctx, wsh)
        flight = Flight(self.remote(n, src, dst, ctx, wsh), landing, sends, receives)
        self.sent.append(flight)
        return flight

    def local(self, src, dst):
        n = self.used
        self.used += 1
        copy = pltpu.make_async_copy(src, dst, self.send_sem.at[n])
        copy.start()
        return copy

    def drain(self):
        for flight in self.sent:
            flight.wait_send()
        self.sent = []


class CtxGather:
    def __init__(self, links, own, buffer, ctx, wsh, count, halves):
        self.links, self.own, self.buffer, self.ctx, self.wsh = links, own, buffer, ctx, wsh
        rows = buffer.shape[1] // halves
        self.spans = [pl.ds(h * rows, rows) for h in range(halves)]
        order = bits_of(count)
        self.orders = [order, order[1::-1] + order[2:]][:halves]
        self.have = [{0: None} for _ in self.spans]
        self.step = 0
        self.steps = len(order)

    def advance(self):
        for h, span in enumerate(self.spans):
            bit = self.orders[h][self.step]
            new = {}
            for offset, arrival in self.have[h].items():
                if arrival is not None:
                    arrival.wait_recv()
                    self.have[h][offset] = None
                block = flip(self.ctx, offset)
                src = self.own.at[span] if offset == 0 else self.buffer.at[block, span]
                new[offset ^ bit] = self.links.send(
                    src, self.buffer.at[block, span], flip(self.ctx, bit), self.wsh
                )
            self.have[h].update(new)
        self.step += 1

    def need(self, offset):
        for have in self.have:
            if have[offset] is not None:
                have[offset].wait_recv()
                have[offset] = None


class WeightGather:
    def __init__(self, links, shard, whole, place, zs, pair):
        self.links, self.shard, self.whole = links, shard, whole
        self.ctx, self.z, self.core = place
        self.zs, self.pair = zs, pair
        self.rows, self.columns = shard.shape
        self.moving, self.from_pair, self.from_core = {}, [], []

    def row_span(self, z, core):
        return pl.ds(pl.multiple_of((z * 2 + core) * self.rows, 16), self.rows)

    def side(self, mine):
        if self.pair is None:
            return pl.ds(0, self.columns)
        half = self.columns // 2
        side = (self.ctx // self.pair) % 2
        if not mine:
            side = 1 - side
        return pl.ds(pl.multiple_of(side * half, LANES), half)

    def away(self, way, hop):
        return (self.z - way * hop + 2 * self.zs) % self.zs

    def arrives(self, way, hop):
        return self.z >= hop if way > 0 else self.z + hop < self.zs

    def can_send(self, way):
        return self.z + 1 < self.zs if way > 0 else self.z > 0

    def forward(self, way, hop, src):
        mine = self.side(True)
        here = self.away(way, hop)
        sends = self.can_send(way)
        if hop > 0:
            sends = jnp.logical_and(sends, self.arrives(way, hop))
        self.moving[way, hop + 1] = self.links.send(
            src,
            self.whole.at[self.row_span(here, self.core), mine],
            self.ctx,
            self.away(way, -1) * 2 + self.core,
            landing=self.whole.at[self.row_span(self.away(way, hop + 1), self.core), mine],
            sends=sends,
            receives=self.arrives(way, hop + 1),
        )

    def start(self):
        rows = self.row_span(self.z, self.core)
        for way in (1, -1):
            self.forward(way, 0, self.shard.at[:, self.side(True)])
        self.from_core.append(
            self.links.send(
                self.shard, self.whole.at[rows], self.ctx, self.z * 2 + 1 - self.core
            )
        )
        self.own = self.links.local(self.shard, self.whole.at[rows])

    def to_core(self, z, span, condition):
        part = self.whole.at[self.row_span(z, self.core), span]
        back = self.whole.at[self.row_span(z, 1 - self.core), span]
        self.from_core.append(
            self.links.send(
                part,
                part,
                self.ctx,
                self.z * 2 + 1 - self.core,
                landing=back,
                sends=condition,
                receives=condition,
            )
        )

    def hop(self, hop):
        mine = self.side(True)
        for way in (1, -1):
            self.moving.pop((way, hop)).wait_recv()
            z = self.away(way, hop)
            part = self.whole.at[self.row_span(z, self.core), mine]
            condition = self.arrives(way, hop)
            if hop + 1 < self.zs:
                self.forward(way, hop, part)
            if self.pair is not None:
                flight = self.links.send(
                    part,
                    part,
                    flip(self.ctx, self.pair),
                    self.z * 2 + self.core,
                    landing=self.whole.at[self.row_span(z, self.core), self.side(False)],
                    sends=condition,
                    receives=condition,
                )
                self.from_pair.append((z, condition, flight))
            self.to_core(z, mine, condition)

    def take_pair(self):
        for z, condition, flight in self.from_pair:
            flight.wait_recv()
            self.to_core(z, self.side(False), condition)
        self.from_pair = []

    def finish(self):
        self.own.wait()
        for flight in self.from_core:
            flight.wait_recv()


class GradScatter:
    def __init__(self, links, whole, final, buffers, place, zs, ctxs, pair):
        self.links, self.whole, self.final = links, whole, final
        self.from_core, self.from_pair, self.from_z, self.from_ctx, self.other = buffers
        self.ctx, self.z, self.core = place
        self.zs, self.pair = zs, pair
        self.rows, self.columns = whole.shape[0] // (2 * zs), whole.shape[1]
        self.cbits = [b for b in bits_of(ctxs) if b != pair]
        self.order = list(range(1, zs)) + [0]

    def span(self, offset, core):
        first = (flip(self.z, offset) * 2 + core) * self.rows
        return pl.ds(pl.multiple_of(first, 16), self.rows)

    def side(self, mine):
        if self.pair is None:
            return pl.ds(0, self.columns)
        half = self.columns // 2
        side = (self.ctx // self.pair) % 2
        if not mine:
            side = 1 - side
        return pl.ds(pl.multiple_of(side * half, LANES), half)

    def wsh_of(self, offset, core):
        return flip(self.z, offset) * 2 + core

    def send_core(self):
        self.flights = []
        for offset in self.order:
            self.flights.append(
                self.links.send(
                    self.whole.at[self.span(offset, 1 - self.core)],
                    self.from_core.at[offset],
                    self.ctx,
                    self.wsh_of(0, 1 - self.core),
                )
            )

    def add(self, offset, columns, others):
        first = (flip(self.z, offset) * 2 + self.core) * self.rows
        piece = 48

        def body(i, carry):
            here = pl.ds(pl.multiple_of(first + i * piece, 16), piece)
            there = pl.ds(pl.multiple_of(i * piece, 16), piece)
            total = self.whole[here, columns].astype(f32)
            for other in others:
                total = total + other[there, :].astype(f32)
            self.whole[here, columns] = total.astype(bf16)
            return carry

        lax.fori_loop(0, self.rows // piece, body, 0)

    def send_pair(self, offset):
        columns = self.side(False)
        return self.links.send(
            self.whole.at[self.span(offset, self.core), columns],
            self.from_pair.at[offset],
            flip(self.ctx, self.pair),
            self.wsh_of(0, self.core),
        )

    def send_z(self, offset):
        columns = self.side(True)
        return self.links.send(
            self.whole.at[self.span(offset, self.core), columns],
            self.from_z.at[offset - 1],
            self.ctx,
            self.wsh_of(offset, self.core),
        )

    def steps(self):
        along_z = {}
        in_pair = {}
        for offset, flight in zip(self.order, self.flights):
            flight.wait_recv()
            self.add(offset, pl.ds(0, self.columns), [self.from_core.at[offset]])
            if self.pair is not None:
                in_pair[offset] = self.send_pair(offset)
            elif offset > 0:
                along_z[offset] = self.send_z(offset)
        yield
        mine = self.side(True)
        for offset, flight in in_pair.items():
            flight.wait_recv()
            self.add(offset, mine, [self.from_pair.at[offset]])
            if offset > 0:
                along_z[offset] = self.send_z(offset)
        if self.pair is not None:
            yield
        for flight in along_z.values():
            flight.wait_recv()
        self.add(0, mine, [self.from_z.at[offset - 1] for offset in along_z])
        half = self.columns // 2
        if self.pair is None:
            parts = [(pl.ds(0, half), self.cbits), (pl.ds(half, half), self.cbits[::-1])]
        else:
            parts = [(mine, self.cbits)]
        for step in range(len(self.cbits)):
            flights = []
            for columns, order in parts:
                there = columns if self.pair is None else pl.ds(0, half)
                flights.append(
                    self.links.send(
                        self.whole.at[self.span(0, self.core), columns],
                        self.from_ctx.at[step, :, there],
                        flip(self.ctx, order[step]),
                        self.wsh_of(0, self.core),
                    )
                )
            yield
            for flight in flights:
                flight.wait_recv()
                flight.wait_send()
            self.add(0, mine, [self.from_ctx.at[step]])
        done = self.whole.at[self.span(0, self.core), mine]
        self.results = [self.links.local(done, self.final.at[:, mine])]
        if self.pair is not None:
            flight = self.links.send(
                done, self.other, flip(self.ctx, self.pair), self.wsh_of(0, self.core)
            )
            yield
            flight.wait_recv()
            self.results.append(self.links.local(self.other, self.final.at[:, self.side(False)]))
        yield


class TableSum:
    def __init__(self, links, table, slots, place, zs, ctxs):
        self.links, self.table, self.slots = links, table, slots
        ctx, z, core = place
        self.hops = (
            [[(ctx, z * 2 + 1 - core)]]
            + [[(ctx, flip(z, o) * 2 + core) for o in range(1, zs)]]
            + [[(flip(ctx, b), z * 2 + core)] for b in bits_of(ctxs)]
        )

    def steps(self):
        slot = 0
        for peers in self.hops:
            flights = []
            for n, peer in enumerate(peers):
                flights.append(
                    self.links.send(self.table, self.slots.at[slot + n], *peer)
                )
            yield
            total = self.table[...]
            for n, flight in enumerate(flights):
                flight.wait_recv()
                flight.wait_send()
                total = total + self.slots[slot + n]
            self.table[...] = total
            slot += len(peers)
        yield


def layer_kernel(
    ctxs,
    zs,
    pairs,
    back_pairs,
    tok,
    cot,
    order,
    order_block,
    vec_0,
    vec_1,
    vec_2,
    vec_3,
    vec_4,
    vec_5,
    vec_6,
    vec_7,
    vec_8,
    qkv_shard,
    out_shard,
    up_shard,
    down_shard,
    home_out,
    home_grad,
    sum_qkv,
    sum_out,
    sum_up,
    sum_down,
    sum_768,
    sum_wide,
    all_tok,
    all_cot,
    all_out,
    all_grad,
    order_column,
    vectors,
    all_order,
    all_vectors,
    w_qkv,
    w_out,
    w_up,
    w_down,
    g_down,
    stage,
    acc,
    inputs,
    low,
    top,
    qkv,
    probs,
    context,
    turned,
    first_norm,
    first_factor,
    hidden,
    slope,
    grad_wide,
    grad_low,
    result_low,
    back_low,
    rows_768,
    row_up,
    small,
    small_slots,
    *rest,
):
    buffers = [rest[5 * n : 5 * n + 5] for n in range(4)]
    send_sem, recv_sem = rest[20:22]
    vec_parts = rest[22:]
    rows, width = tok.shape
    wide = up_shard.shape[1]
    pairs_of_heads = width // LANES
    blocks = rows // CLUSTER
    scale = HEAD_DIM**-0.5
    ctx = lax.axis_index("ctx")
    wsh = lax.axis_index("wsh")
    z, core = wsh // 2, wsh % 2
    place = (ctx, z, core)
    links = Links(send_sem, recv_sem)

    brought = [
        links.local(vector, vec_parts[n])
        for n, vector in enumerate(
            (vec_0, vec_1, vec_2, vec_3, vec_4, vec_5, vec_6, vec_7, vec_8)
        )
    ]
    vectors[...] = jnp.zeros_like(vectors)
    for n, copy in enumerate(brought):
        copy.wait()
        vectors[n : n + 1, 0 : vec_parts[n].shape[0]] = vec_parts[n][...].reshape(1, -1)
    order_column[...] = (
        jnp.broadcast_to(order[...].astype(f32), (LANES, rows)).T.astype(jnp.int32)
    )

    barrier = pltpu.get_barrier_semaphore()
    stream_peers = [
        (ctx, flip(z, o) * 2 + (core if same else 1 - core))
        for o in range(zs)
        for same in (True, False)
        if o > 0 or not same
    ]
    peers = stream_peers + [(flip(ctx, b), wsh) for b in bits_of(ctxs)]
    for peer in peers:
        pl.semaphore_signal(barrier, 1, device_id=peer, device_id_type=pl.DeviceIdType.MESH)
    pl.semaphore_wait(barrier, len(peers))

    tok_gather = CtxGather(links, tok, all_tok, ctx, wsh, ctxs, 2)
    cot_gather = CtxGather(links, cot, all_cot, ctx, wsh, ctxs, 2)
    order_gather = CtxGather(links, order_block, all_order, ctx, wsh, ctxs, 1)
    vec_own = links.local(vectors, all_vectors.at[wsh])
    vec_flights = [links.send(vectors, all_vectors.at[wsh], *peer) for peer in stream_peers]
    q_gather, o_gather, u_gather, d_gather = [
        WeightGather(links, s, w, place, zs, p)
        for s, w, p in zip(
            (qkv_shard, out_shard, up_shard, down_shard), (w_qkv, w_out, w_up, w_down), pairs
        )
    ]
    tok_gather.advance()
    order_gather.advance()
    q_gather.start()
    o_gather.start()
    q_gather.hop(1)
    o_gather.hop(1)
    u_gather.start()
    while tok_gather.step < tok_gather.steps:
        tok_gather.advance()
        order_gather.advance()
    for hop in range(2, zs):
        q_gather.hop(hop)
        o_gather.hop(hop)
    cot_gather.advance()
    vec_own.wait()
    for flight in vec_flights:
        flight.wait_recv()

    rows_768[...] = jnp.zeros_like(rows_768)
    row_up[...] = jnp.zeros_like(row_up)
    length = width // (2 * zs)

    def spread(part, spot, size, target):
        first = min(spot // LANES * LANES, target.shape[1] - 2 * part.shape[1])
        shape = (part.shape[1], 2 * part.shape[1])
        j = lax.broadcasted_iota(jnp.int32, shape, 0)
        col = lax.broadcasted_iota(jnp.int32, shape, 1)
        move = jnp.where((col == j + (spot - first)) & (j < size), 1.0, 0.0).astype(bf16)
        at = pl.ds(first, shape[1])
        target[:, at] = target[:, at] + mm(part, move)[: target.shape[0]]

    length_up = wide // (2 * zs)
    for s in range(2 * zs):
        spread(all_vectors[s, :, 0:LANES], length * s, length, rows_768)
        if length_up % LANES == 0:
            up_part = all_vectors[s, 8:16, 0:length_up].astype(f32)
            row_up[0:1, length_up * s : length_up * (s + 1)] = up_part[0:1]
        else:
            spread(all_vectors[s, 8:16, :], length_up * s, length_up, row_up)

    def pick(gather, own, total):
        copies = {}

        def fetch(offset):
            if offset == 0:
                src = own
            else:
                gather.need(offset)
                src = gather.buffer.at[flip(ctx, offset)]
            copies[offset] = links.local(src, stage.at[offset % 2])

        fetch(0)
        for offset in range(ctxs):
            copies[offset].wait()
            if offset + 1 < ctxs:
                fetch(offset + 1)
            first = flip(ctx, offset) * rows

            def body(i, carry):
                here = pl.ds(pl.multiple_of(i * CLUSTER, CLUSTER), CLUSTER)
                place_of = order_column[here, :]
                lane = lax.broadcasted_iota(jnp.int32, (CLUSTER, LANES), 1)
                chosen = jnp.concatenate(
                    [
                        jnp.where(place_of == lane + (first + t * LANES), 1.0, 0.0).astype(bf16)
                        for t in range(rows // LANES)
                    ],
                    axis=1,
                )
                got = mm(chosen, stage[offset % 2])
                total[here, :] = got if offset == 0 else total[here, :] + got
                return carry

            lax.fori_loop(0, blocks, body, 0)

    def bring_home(gather, own, target):
        copies = {}

        def fetch(offset):
            if offset == 0:
                src = own
            else:
                gather.need(offset)
                src = gather.buffer.at[flip(ctx, offset)]
            copies[offset] = links.local(src, stage.at[offset % 2])

        fetch(0)
        for offset in range(ctxs):
            copies[offset].wait()
            if offset + 1 < ctxs:
                fetch(offset + 1)
            if offset == 0:
                places = order[...]
            else:
                order_gather.need(offset)
                places = all_order[flip(ctx, offset)]

            def body(i, carry):
                here = pl.ds(pl.multiple_of(i * CLUSTER, CLUSTER), CLUSTER)
                token = lax.broadcasted_iota(jnp.int32, (CLUSTER, rows), 0) + (
                    ctx * rows + i * CLUSTER
                )
                chosen = jnp.where(places[0:1, :] == token, 1.0, 0.0).astype(bf16)
                got = mm(chosen, stage[offset % 2])
                if offset > 0:
                    got = acc[here, :] + got
                if offset == ctxs - 1:
                    target[here, :] = got.astype(bf16)
                else:
                    acc[here, :] = got
                return carry

            lax.fori_loop(0, blocks, body, 0)

    def tiles(columns, body, first=0):
        def step(t, carry):
            body(t, pl.ds(pl.multiple_of(t * STEP, STEP), STEP))
            return carry

        lax.fori_loop(first // STEP, columns // STEP, step, 0)

    def row_pass(size, body):
        def step(i, carry):
            body(pl.ds(pl.multiple_of(i * size, size), size))
            return carry

        lax.fori_loop(0, rows // size, step, 0)

    def tally(vector, values):
        total = jnp.sum(values, axis=0, keepdims=True)
        for t in range(width // STEP):
            at = pl.ds(vector * (width // STEP) + t, 1)
            small[at, :] = small[at, :] + total[:, t * STEP : (t + 1) * STEP]

    small[...] = jnp.zeros_like(small)
    qbias, vbias, obias, gain1, shift1, dbias, gain2, shift2 = [
        rows_768.at[pl.ds(n, 1)] for n in range(8)
    ]

    u_gather.hop(1)
    d_gather.start()
    pick(tok_gather, tok, acc)

    def keep_inputs(here):
        inputs[here, :] = acc[here, :].astype(bf16)

    row_pass(CLUSTER, keep_inputs)
    u_gather.hop(2)
    q_gather.take_pair()
    o_gather.take_pair()
    q_gather.finish()

    def project(t, span):
        at = pl.ds(pl.multiple_of((t % (width // STEP)) * STEP, STEP), STEP)
        part = t // (width // STEP)
        bias = jnp.where(part == 0, qbias[:, at], jnp.where(part == 2, vbias[:, at], 0.0))
        qkv[:, span] = (mm(inputs[...], w_qkv[:, span]) + bias).astype(bf16)

    tiles(3 * width, project)

    d_gather.hop(1)
    cot_gather.advance()

    lane = lax.broadcasted_iota(jnp.int32, (1, LANES), 1)
    left = jnp.where(lane < HEAD_DIM, 1.0, 0.0).astype(bf16)
    right = jnp.where(lane < HEAD_DIM, 0.0, 1.0).astype(bf16)

    def both(values):
        return jnp.concatenate([values * left, values * right], axis=0)

    def side_by_side(values):
        return jnp.concatenate([values[:CLUSTER], values[CLUSTER:]], axis=1)

    def part_of(here, kind, pair):
        return qkv[here, kind * width + pair * LANES : kind * width + (pair + 1) * LANES]

    def attend(b, carry):
        here = pl.ds(pl.multiple_of(b * CLUSTER, CLUSTER), CLUSTER)
        visible = order[0:1, here] <= order_column[here, :]
        hide = jnp.where(visible, 0.0, -1e30)
        hide = jnp.concatenate([hide, hide], axis=0)
        for pair in range(pairs_of_heads):
            query, keyed, valued = [part_of(here, kind, pair) for kind in range(3)]
            scores = mm_nt(both(query), keyed) * scale + hide
            expd = jnp.exp(scores - jnp.max(scores, axis=1, keepdims=True))
            prob = expd * (1.0 / jnp.sum(expd, axis=1, keepdims=True))
            probs[b * pairs_of_heads + pair] = prob
            got = mm(side_by_side(prob.astype(bf16)), both(valued))
            context[here, pair * LANES : (pair + 1) * LANES] = got.astype(bf16)
        return carry

    lax.fori_loop(0, blocks, attend, 0)
    for hop in range(3, zs):
        u_gather.hop(hop)
    o_gather.finish()

    def out_project(t, span):
        acc[:, span] = mm(context[...], w_out[:, span])

    tiles(width, out_project)

    def first_normalize(here):
        attended = (acc[here, :] + obias[...]).astype(bf16).astype(f32)
        resid = inputs[here, :].astype(f32) + attended
        centre = resid - jnp.mean(resid, axis=1, keepdims=True)
        factor = lax.rsqrt(jnp.mean(centre * centre, axis=1, keepdims=True) + epsilon)
        normed = centre * factor
        first_norm[here, :] = normed
        first_factor[here, :] = factor
        low[here, :] = (normed * gain1[...] + shift1[...]).astype(bf16)

    row_pass(64, first_normalize)
    u_gather.take_pair()
    while cot_gather.step < cot_gather.steps:
        cot_gather.advance()
    u_gather.finish()

    def feed(t, span):
        pre = mm(low[...], w_up[:, span]) + row_up[0:1, span]
        half = 0.5 * (1.0 + lax.erf(pre * 0.7071067811865476))
        hidden[:, span] = (pre * half).astype(bf16)
        slope[:, span] = (half + pre * jnp.exp(-0.5 * pre * pre) * 0.3989422804014327).astype(bf16)

    tiles(wide, feed)
    d_gather.hop(2)
    pick(cot_gather, cot, acc)

    def keep_top(here):
        top[here, :] = acc[here, :].astype(bf16)

    row_pass(CLUSTER, keep_top)
    for hop in range(3, zs):
        d_gather.hop(hop)
    d_gather.take_pair()
    d_gather.finish()

    def down(t, span):
        acc[:, span] = mm(hidden[...], w_down[:, span])

    tiles(width, down)

    def second_normalize(here):
        first_out = first_norm[here, :] * gain1[...] + shift1[...]
        second_in = first_out + acc[here, :] + dbias[...]
        centre = second_in - jnp.mean(second_in, axis=1, keepdims=True)
        factor = lax.rsqrt(jnp.mean(centre * centre, axis=1, keepdims=True) + epsilon)
        normed = centre * factor
        result_low[here, :] = (normed * gain2[...] + shift2[...]).astype(bf16)
        grad_top = top[here, :].astype(f32)
        tally(6, grad_top * normed)
        tally(7, grad_top)
        grad_normed = grad_top * gain2[...]
        grad = factor * (
            grad_normed
            - jnp.mean(grad_normed, axis=1, keepdims=True)
            - normed * jnp.mean(grad_normed * normed, axis=1, keepdims=True)
        )
        grad_wide[here, :] = grad
        grad = grad.astype(bf16)
        grad_low[here, :] = grad
        tally(5, grad.astype(f32))

    row_pass(64, second_normalize)

    scatters = [
        GradScatter(links, w, f, b, place, zs, ctxs, p)
        for w, f, b, p in zip(
            (w_qkv, w_out, w_up, g_down),
            (sum_qkv, sum_out, sum_up, sum_down),
            buffers,
            back_pairs,
        )
    ]
    gathered, links.sent = links.sent, []
    out_gather = CtxGather(links, result_low, all_out, ctx, wsh, ctxs, 2)
    out_gather.advance()
    part_rows = wide // (2 * zs)

    def down_grad(owner):
        def body(i, carry):
            here = pl.ds(pl.multiple_of((i * 2 + owner) * part_rows, LANES // 2), part_rows)
            turned_hidden = hidden_turned(i * 2 + owner)
            g_down[here, :] = mm(turned_hidden, grad_low[...]).astype(bf16)
            return carry

        lax.fori_loop(0, zs, body, 0)

    if part_rows % LANES == 0:

        def hidden_turned(s):
            return hidden[:, pl.ds(pl.multiple_of(s * part_rows, LANES), part_rows)].T

        down_grad(1 - core)
        scatters[3].send_core()
        down_grad(core)
    else:

        def all_down(t, span):
            g_down[span, :] = mm(hidden[:, span].T, grad_low[...]).astype(bf16)

        tiles(wide, all_down)
        scatters[3].send_core()

    def back_hidden(t, span):
        grad = (mm_nt(grad_low[...], w_down[span, :]) * slope[:, span]).astype(bf16)
        slope[:, span] = grad
        small[pl.ds(8 * (width // STEP) + t, 1), :] = jnp.sum(
            grad.astype(f32), axis=0, keepdims=True
        )

    tiles(wide // 2, back_hidden)
    down_steps = scatters[3].steps()
    next(down_steps)
    tiles(wide, back_hidden, wide // 2)

    def back_up(t, span):
        acc[:, span] = mm_nt(slope[...], w_up[span, :])

    tiles(width, back_up)

    def first_back(here):
        grad_first = grad_wide[here, :] + acc[here, :]
        normed = first_norm[here, :]
        tally(3, grad_first * normed)
        tally(4, grad_first)
        grad_normed = grad_first * gain1[...]
        grad = first_factor[here, :] * (
            grad_normed
            - jnp.mean(grad_normed, axis=1, keepdims=True)
            - normed * jnp.mean(grad_normed * normed, axis=1, keepdims=True)
        )
        grad_wide[here, :] = grad
        grad = grad.astype(bf16)
        grad_low[here, :] = grad
        tally(2, grad.astype(f32))

    row_pass(64, first_back)
    while out_gather.step < out_gather.steps:
        out_gather.advance()
    for flight in gathered:
        flight.wait_send()

    turned[...] = low[...].T

    def up_grad(t, span):
        w_up[:, span] = mm(turned[...], slope[:, span]).astype(bf16)

    tiles(wide, up_grad)
    scatters[2].send_core()

    turned[...] = context[...].T

    def back_context(t, span):
        context[:, span] = mm_nt(grad_low[...], w_out[span, :]).astype(bf16)

    tiles(width, back_context)

    def out_grad(t, span):
        w_out[:, span] = mm(turned[...], grad_low[:, span]).astype(bf16)

    tiles(width, out_grad)
    scatters[1].send_core()
    up_steps = scatters[2].steps()
    next(up_steps)
    out_steps = scatters[1].steps()
    next(out_steps)

    def back_attend(b, carry):
        here = pl.ds(pl.multiple_of(b * CLUSTER, CLUSTER), CLUSTER)
        for pair in range(pairs_of_heads):
            query, keyed, valued = [part_of(here, kind, pair) for kind in range(3)]
            prob = probs[b * pairs_of_heads + pair]
            grad = both(context[here, pair * LANES : (pair + 1) * LANES])
            grad_prob = mm_nt(grad, valued)
            grad_valued = mm_tn(prob.astype(bf16), grad)
            inner = jnp.sum(prob * grad_prob, axis=1, keepdims=True)
            grad_score = (prob * (grad_prob - inner)).astype(bf16)
            grad_query = mm(side_by_side(grad_score), both(keyed)) * scale
            grad_keyed = mm_tn(grad_score, both(query)) * scale
            for kind, value in enumerate((grad_query, grad_keyed, grad_valued)):
                at = kind * width + pair * LANES
                qkv[here, at : at + LANES] = value.astype(bf16)
        return carry

    lax.fori_loop(0, blocks, back_attend, 0)

    def input_sums(here):
        tally(0, qkv[here, 0:width].astype(f32))
        tally(1, qkv[here, 2 * width : 3 * width].astype(f32))

    row_pass(64, input_sums)

    def back_qkv(t, span):
        back_low[:, span] = (mm_nt(qkv[...], w_qkv[span, :]) + grad_wide[:, span]).astype(bf16)

    tiles(width, back_qkv)
    grad_gather = CtxGather(links, back_low, all_grad, ctx, wsh, ctxs, 2)
    turned[...] = inputs[...].T

    def qkv_grad(t, span):
        w_qkv[:, span] = mm(turned[...], qkv[:, span]).astype(bf16)

    tiles(3 * width, qkv_grad)
    scatters[0].send_core()
    table = TableSum(links, small, small_slots, place, zs, ctxs)
    table_steps = table.steps()
    next(table_steps)
    next(out_steps)
    bring_home(out_gather, result_low, home_out)
    qkv_steps = scatters[0].steps()
    next(qkv_steps)
    grad_gather.advance()
    next(table_steps)
    next(up_steps)
    while grad_gather.step < grad_gather.steps:
        grad_gather.advance()
    next(down_steps)
    next(qkv_steps)
    next(down_steps)
    next(out_steps)
    next(table_steps)
    next(down_steps)
    next(out_steps)
    next(up_steps)
    bring_home(grad_gather, back_low, home_grad)
    running = [down_steps, out_steps, up_steps, table_steps, qkv_steps]
    while running:
        still = []
        for steps in running:
            if next(steps, "end") != "end":
                still.append(steps)
        running = still
    count = width // STEP
    for n in range(8):
        for t in range(count):
            sum_768[n : n + 1, t * STEP : (t + 1) * STEP] = small[n * count + t : n * count + t + 1]
    for t in range(wide // STEP):
        sum_wide[0:1, t * STEP : (t + 1) * STEP] = small[8 * count + t : 8 * count + t + 1]
    links.drain()
    for scatter in scatters:
        for result in scatter.results:
            result.wait()


def finish_kernel(wshs, *refs):
    sources, (sum_768, sum_wide) = refs[:6], refs[6:8]
    targets, vecs = refs[8:14], refs[14:23]
    taken, given, sem = refs[23:29], refs[29:35], refs[35]
    coming = [pltpu.make_async_copy(s, t, sem.at[n]) for n, (s, t) in enumerate(zip(sources, taken))]
    for copy in coming:
        copy.start()
    me = lax.axis_index("wsh")
    for sums, outs in ((sum_768, vecs[:8]), (sum_wide, vecs[8:])):
        size = outs[0].shape[0]
        columns = sums.shape[1]
        mine = pltpu.roll(sums[...], lax.rem(columns - me * size, columns), 1)
        for n, out in enumerate(outs):
            out[...] = mine[n, 0:size]
    going = []
    for n, copy in enumerate(coming):
        copy.wait()
        given[n][...] = taken[n][...].astype(given[n].dtype)
        going.append(pltpu.make_async_copy(given[n], targets[n], sem.at[6 + n]))
        going[-1].start()
    for copy in going:
        copy.wait()


def on_device(
    ctxs,
    wshs,
    tokens,
    cluster_order,
    qkv_weight,
    query_bias,
    value_bias,
    out_weight,
    out_bias,
    first_gain,
    first_shift,
    up_weight,
    up_bias,
    down_weight,
    down_bias,
    second_gain,
    second_shift,
    cotangent,
):
    rows, width = tokens.shape[1:]
    wide = up_weight.shape[1]
    zs = wshs // 2
    small_rows = 8 * (width // STEP) + wide // STEP
    small_rows = (small_rows + 7) // 8 * 8
    vector_lanes = (up_bias.shape[0] + LANES - 1) // LANES * LANES
    heads_pairs = width // LANES
    blocks = rows // CLUSTER
    hops = zs + len(bits_of(ctxs))
    shards = [qkv_weight.shape, out_weight.shape, up_weight.shape, down_weight.shape]
    sems = 2 * wshs + 4 * 2 * ctxs * 2 + 10 * zs * 4 + 4 * (4 * zs + 8) + 64

    def vmem(shape, dtype=bf16):
        return pltpu.VMEM(shape, dtype)

    pairs = (1, 1, 2, None)
    back_pairs = (2, 2, 1, None)
    landing = []
    for (n, columns), pair in zip(shards, back_pairs):
        part = columns // 2
        landing.append(vmem((zs, n, columns)))
        if pair is None:
            landing.append(vmem((1, 16, LANES)))
            landing.append(vmem((zs - 1, n, columns)))
            landing.append(vmem((len(bits_of(ctxs)), n, columns)))
            landing.append(vmem((16, LANES)))
        else:
            landing.append(vmem((zs, n, part)))
            landing.append(vmem((zs - 1, n, part)))
            landing.append(vmem((len(bits_of(ctxs)) - 1, n, part)))
            landing.append(vmem((n, part)))
    anywhere = pl.BlockSpec(memory_space=pl.ANY)
    on_chip = pl.BlockSpec(memory_space=pltpu.VMEM)
    many = jax.ShapeDtypeStruct((ctxs, rows, width), bf16)
    results = pl.pallas_call(
        functools.partial(layer_kernel, ctxs, zs, pairs, back_pairs),
        out_shape=[
            jax.ShapeDtypeStruct((rows, width), bf16),
            jax.ShapeDtypeStruct((rows, width), bf16),
        ]
        + [jax.ShapeDtypeStruct(s, bf16) for s in shards]
        + [jax.ShapeDtypeStruct((8, width), f32), jax.ShapeDtypeStruct((8, wide), f32)]
        + [many] * 4,
        in_specs=[anywhere, anywhere, on_chip, anywhere] + [anywhere] * 13,
        out_specs=[on_chip, on_chip] + [anywhere] * 4 + [on_chip] * 2 + [anywhere] * 4,
        scratch_shapes=[
            vmem((rows, LANES), jnp.int32),
            vmem((16, vector_lanes)),
            vmem((ctxs, 1, rows), jnp.int32),
            vmem((wshs, 16, vector_lanes)),
            vmem((width, 3 * width)),
            vmem((width, width)),
            vmem((width, wide)),
            vmem((wide, width)),
            vmem((wide, width)),
            vmem((2, rows, width)),
            vmem((rows, width), f32),
            vmem((rows, width)),
            vmem((rows, width)),
            vmem((rows, width)),
            vmem((rows, 3 * width)),
            vmem((blocks * heads_pairs, 2 * CLUSTER, CLUSTER), f32),
            vmem((rows, width)),
            vmem((width, rows)),
            vmem((rows, width), f32),
            vmem((rows, 1), f32),
            vmem((rows, wide)),
            vmem((rows, wide)),
            vmem((rows, width), f32),
            vmem((rows, width)),
            vmem((rows, width)),
            vmem((rows, width)),
            vmem((8, width), f32),
            vmem((8, wide), f32),
            vmem((small_rows, STEP), f32),
            vmem((hops, small_rows, STEP), f32),
        ]
        + landing
        + [pltpu.SemaphoreType.DMA((sems,)), pltpu.SemaphoreType.DMA((sems,))]
        + [vmem(query_bias.shape)] * 8
        + [vmem(up_bias.shape)],
        compiler_params=pltpu.CompilerParams(
            collective_id=0, has_side_effects=True, vmem_limit_bytes=67043328
        ),
        name="layer",
    )(
        tokens[0],
        cotangent[0],
        cluster_order,
        cluster_order,
        query_bias,
        value_bias,
        out_bias,
        first_gain,
        first_shift,
        down_bias,
        second_gain,
        second_shift,
        up_bias,
        qkv_weight,
        out_weight,
        up_weight,
        down_weight,
    )
    big = results[:6]
    part = width // wshs
    part_wide = wide // wshs
    outs = [jax.ShapeDtypeStruct((rows, width), bf16), jax.ShapeDtypeStruct((rows, width), f32)]
    outs += [jax.ShapeDtypeStruct(s, f32) for s in shards]
    outs += [jax.ShapeDtypeStruct((part,), f32)] * 8 + [jax.ShapeDtypeStruct((part_wide,), f32)]
    (home_out, home_grad, g_qkv, g_out, g_up, g_down, *vecs) = pl.pallas_call(
        functools.partial(finish_kernel, wshs),
        out_shape=outs,
        in_specs=[anywhere] * 6 + [on_chip] * 2,
        out_specs=[anywhere] * 6 + [on_chip] * 9,
        scratch_shapes=[vmem(v.shape) for v in big]
        + [vmem(v.shape, o.dtype) for v, o in zip(big, outs)]
        + [pltpu.SemaphoreType.DMA((12,))],
        compiler_params=pltpu.CompilerParams(vmem_limit_bytes=67043328),
        name="finish",
    )(*big, *results[6:8])
    g_q, g_v, g_o, g_g1, g_s1, g_d, g_g2, g_s2, g_u = vecs
    return (
        home_out[None],
        home_grad[None],
        g_qkv,
        g_q,
        g_v,
        g_out,
        g_o,
        g_g1,
        g_s1,
        g_up,
        g_u,
        g_down,
        g_d,
        g_g2,
        g_s2,
    )


def solution(mesh):
    row = P("wsh", None)
    vec = P("wsh")
    seq = P("wsh", "ctx", None)
    in_specs = (
        seq,
        P("wsh", "ctx"),
        row,
        vec,
        vec,
        row,
        vec,
        vec,
        vec,
        row,
        vec,
        row,
        vec,
        vec,
        vec,
        seq,
    )
    out_specs = (
        seq,
        seq,
        row,
        vec,
        vec,
        row,
        vec,
        vec,
        vec,
        row,
        vec,
        row,
        vec,
        vec,
        vec,
    )
    return jax.shard_map(
        functools.partial(on_device, mesh.shape["ctx"], mesh.shape["wsh"]),
        mesh=mesh,
        in_specs=in_specs,
        out_specs=out_specs,
        check_vma=False,
    )
```

```python
import functools

import jax
import jax.numpy as jnp
from jax import lax
from jax.experimental import pallas as pl
from jax.experimental.pallas import tpu as pltpu
from jax.sharding import PartitionSpec as P

HEAD_DIM = 64
CLUSTER = 128
LANES = 128
STEP = 256

epsilon = 1e-05
bf16 = jnp.bfloat16
f32 = jnp.float32


def mm(left, right):
    return lax.dot_general(left, right, (((1,), (0,)), ((), ())), preferred_element_type=f32)


def mm_nt(left, right):
    return lax.dot_general(left, right, (((1,), (1,)), ((), ())), preferred_element_type=f32)


def mm_tn(left, right):
    return lax.dot_general(left, right, (((0,), (0,)), ((), ())), preferred_element_type=f32)


def flip(index, offset):
    bit = 1
    result = index
    while bit <= offset:
        if offset & bit:
            result = result + bit * (1 - 2 * ((index // bit) % 2))
        bit *= 2
    return result


def bits_of(size):
    found, bit = [], 1
    while bit < size:
        found.append(bit)
        bit *= 2
    return found


def low_bit(value):
    return value & -value


def only_if(condition, action):
    if condition is None:
        action()
    else:
        pl.when(condition)(action)


class Flight:
    def __init__(self, copy, landing=None, sends=None, receives=None):
        self.copy, self.landing = copy, landing or copy
        self.sends, self.receives = sends, receives
        self.leaving = self.coming = True
        only_if(sends, copy.start)

    def wait_recv(self):
        if self.coming:
            only_if(self.receives, self.landing.wait_recv)
        self.coming = False

    def wait_send(self):
        if self.leaving:
            only_if(self.sends, self.copy.wait_send)
        self.leaving = False


class Links:
    def __init__(self, send_sem, recv_sem):
        self.send_sem, self.recv_sem, self.used = send_sem, recv_sem, 0
        self.sent = []

    def remote(self, n, src, dst, ctx, wsh):
        return pltpu.make_async_remote_copy(
            src_ref=src,
            dst_ref=dst,
            send_sem=self.send_sem.at[n],
            recv_sem=self.recv_sem.at[n],
            device_id=(ctx, wsh),
            device_id_type=pl.DeviceIdType.MESH,
        )

    def send(self, src, dst, ctx, wsh, landing=None, sends=None, receives=None):
        n = self.used
        self.used += 1
        if landing is not None:
            landing = self.remote(n, landing, landing, ctx, wsh)
        flight = Flight(self.remote(n, src, dst, ctx, wsh), landing, sends, receives)
        self.sent.append(flight)
        return flight

    def local(self, src, dst):
        n = self.used
        self.used += 1
        copy = pltpu.make_async_copy(src, dst, self.send_sem.at[n])
        copy.start()
        return copy

    def drain(self):
        for flight in self.sent:
            flight.wait_send()
        self.sent = []


class CtxGather:
    def __init__(self, links, own, buffer, ctx, wsh, count, halves):
        self.links, self.own, self.buffer, self.ctx, self.wsh = links, own, buffer, ctx, wsh
        rows = buffer.shape[1] // halves
        self.spans = [pl.ds(h * rows, rows) for h in range(halves)]
        order = bits_of(count)
        self.orders = [order, order[1::-1] + order[2:]][:halves]
        self.have = [{0: None} for _ in self.spans]
        self.step = 0
        self.steps = len(order)

    def advance(self):
        for h, span in enumerate(self.spans):
            bit = self.orders[h][self.step]
            new = {}
            for offset, arrival in self.have[h].items():
                if arrival is not None:
                    arrival.wait_recv()
                    self.have[h][offset] = None
                block = flip(self.ctx, offset)
                src = self.own.at[span] if offset == 0 else self.buffer.at[block, span]
                new[offset ^ bit] = self.links.send(
                    src, self.buffer.at[block, span], flip(self.ctx, bit), self.wsh
                )
            self.have[h].update(new)
        self.step += 1

    def need(self, offset):
        for have in self.have:
            if have[offset] is not None:
                have[offset].wait_recv()
                have[offset] = None


class WeightGather:
    def __init__(self, links, shard, whole, pair, place, zs):
        self.links, self.shard, self.whole = links, shard, whole
        self.ctx, self.z, self.core = place
        self.zs, self.pair = zs, pair
        self.rows, self.columns = shard.shape
        self.moving, self.from_pair, self.from_core = {}, [], []

    def row_span(self, z, core):
        return pl.ds(pl.multiple_of((z * 2 + core) * self.rows, 16), self.rows)

    def side(self, mine):
        if self.pair is None:
            return pl.ds(0, self.columns)
        half = self.columns // 2
        side = (self.ctx // self.pair) % 2
        if not mine:
            side = 1 - side
        return pl.ds(pl.multiple_of(side * half, LANES), half)

    def away(self, way, hop):
        return (self.z - way * hop + 2 * self.zs) % self.zs

    def arrives(self, way, hop):
        return self.z >= hop if way > 0 else self.z + hop < self.zs

    def can_send(self, way):
        return self.z + 1 < self.zs if way > 0 else self.z > 0

    def forward(self, way, hop, src):
        mine = self.side(True)
        here = self.away(way, hop)
        sends = self.can_send(way)
        if hop > 0:
            sends = jnp.logical_and(sends, self.arrives(way, hop))
        self.moving[way, hop + 1] = self.links.send(
            src,
            self.whole.at[self.row_span(here, self.core), mine],
            self.ctx,
            self.away(way, -1) * 2 + self.core,
            landing=self.whole.at[self.row_span(self.away(way, hop + 1), self.core), mine],
            sends=sends,
            receives=self.arrives(way, hop + 1),
        )

    def start(self):
        rows = self.row_span(self.z, self.core)
        for way in (1, -1):
            self.forward(way, 0, self.shard.at[:, self.side(True)])
        self.from_core.append(
            self.links.send(
                self.shard, self.whole.at[rows], self.ctx, self.z * 2 + 1 - self.core
            )
        )
        self.own = self.links.local(self.shard, self.whole.at[rows])

    def to_core(self, z, span, condition):
        part = self.whole.at[self.row_span(z, self.core), span]
        back = self.whole.at[self.row_span(z, 1 - self.core), span]
        self.from_core.append(
            self.links.send(
                part,
                part,
                self.ctx,
                self.z * 2 + 1 - self.core,
                landing=back,
                sends=condition,
                receives=condition,
            )
        )

    def hop(self, hop):
        mine = self.side(True)
        for way in (1, -1):
            self.moving.pop((way, hop)).wait_recv()
            z = self.away(way, hop)
            part = self.whole.at[self.row_span(z, self.core), mine]
            condition = self.arrives(way, hop)
            if hop + 1 < self.zs:
                self.forward(way, hop, part)
            if self.pair is not None:
                flight = self.links.send(
                    part,
                    part,
                    flip(self.ctx, self.pair),
                    self.z * 2 + self.core,
                    landing=self.whole.at[self.row_span(z, self.core), self.side(False)],
                    sends=condition,
                    receives=condition,
                )
                self.from_pair.append((z, condition, flight))
            self.to_core(z, mine, condition)

    def take_pair(self):
        for z, condition, flight in self.from_pair:
            flight.wait_recv()
            self.to_core(z, self.side(False), condition)
        self.from_pair = []

    def finish(self):
        self.own.wait()
        for flight in self.from_core:
            flight.wait_recv()


class GradScatter:
    def __init__(self, links, whole, final, buffers, place, zs, ctxs, pair):
        self.links, self.whole, self.final = links, whole, final
        self.from_core, self.from_pair, self.from_z, self.from_ctx, self.other = buffers
        self.ctx, self.z, self.core = place
        self.zs, self.pair = zs, pair
        self.rows, self.columns = whole.shape[0] // (2 * zs), whole.shape[1]
        self.cbits = [b for b in bits_of(ctxs) if b != pair]
        self.order = sorted(range(zs), key=lambda o: (-(o % 2), -o))

    def span(self, offset, core):
        first = (flip(self.z, offset) * 2 + core) * self.rows
        return pl.ds(pl.multiple_of(first, 16), self.rows)

    def side(self, mine):
        if self.pair is None:
            return pl.ds(0, self.columns)
        half = self.columns // 2
        side = (self.ctx // self.pair) % 2
        if not mine:
            side = 1 - side
        return pl.ds(pl.multiple_of(side * half, LANES), half)

    def wsh_of(self, offset, core):
        return flip(self.z, offset) * 2 + core

    def send_core(self):
        self.flights = []
        for offset in self.order:
            self.flights.append(
                self.links.send(
                    self.whole.at[self.span(offset, 1 - self.core)],
                    self.from_core.at[offset],
                    self.ctx,
                    self.wsh_of(0, 1 - self.core),
                )
            )

    def add(self, offset, columns, others):
        first = (flip(self.z, offset) * 2 + self.core) * self.rows
        piece = 48

        def body(i, carry):
            here = pl.ds(pl.multiple_of(first + i * piece, 16), piece)
            there = pl.ds(pl.multiple_of(i * piece, 16), piece)
            total = self.whole[here, columns].astype(f32)
            for other in others:
                total = total + other[there, :].astype(f32)
            self.whole[here, columns] = total.astype(bf16)
            return carry

        lax.fori_loop(0, self.rows // piece, body, 0)

    def send_pair(self, offset):
        columns = self.side(False)
        return self.links.send(
            self.whole.at[self.span(offset, self.core), columns],
            self.from_pair.at[offset],
            flip(self.ctx, self.pair),
            self.wsh_of(0, self.core),
        )

    def send_z(self, offset):
        columns = self.side(True)
        return self.links.send(
            self.whole.at[self.span(offset, self.core), columns],
            self.from_z.at[self.slot(low_bit(offset), offset - low_bit(offset))],
            self.ctx,
            self.wsh_of(low_bit(offset), self.core),
        )

    def slot(self, bit, offset):
        first = 0
        for earlier in bits_of(bit):
            first += self.zs // (2 * earlier)
        return first + offset // (2 * bit)

    def steps(self):
        mine = self.side(True)
        coming = {}
        in_pair = {}

        def pass_on(offset):
            if offset > 0:
                coming[offset - low_bit(offset)] = self.send_z(offset)

        for offset, flight in zip(self.order, self.flights):
            flight.wait_recv()
            self.add(offset, pl.ds(0, self.columns), [self.from_core.at[offset]])
            if self.pair is not None:
                in_pair[offset] = self.send_pair(offset)
            elif offset % 2:
                pass_on(offset)
        yield
        for offset, flight in in_pair.items():
            flight.wait_recv()
            self.add(offset, mine, [self.from_pair.at[offset]])
            if offset % 2:
                pass_on(offset)
            yield
        for bit in bits_of(self.zs):
            taken, coming = coming, {}
            for offset in sorted(taken, key=lambda o: -(o % (2 * bit) + (o & (2 * bit)))):
                taken[offset].wait_recv()
                self.add(offset, mine, [self.from_z.at[self.slot(bit, offset)]])
                if offset & (2 * bit):
                    pass_on(offset)
                if offset:
                    yield
            if 2 * bit < self.zs:
                yield
        half = self.columns // 2
        if self.pair is None:
            parts = [(pl.ds(0, half), self.cbits), (pl.ds(half, half), self.cbits[::-1])]
        else:
            parts = [(mine, self.cbits)]
        for step in range(len(self.cbits)):
            flights = []
            for columns, order in parts:
                there = columns if self.pair is None else pl.ds(0, half)
                flights.append(
                    self.links.send(
                        self.whole.at[self.span(0, self.core), columns],
                        self.from_ctx.at[step, :, there],
                        flip(self.ctx, order[step]),
                        self.wsh_of(0, self.core),
                    )
                )
            yield
            for flight in flights:
                flight.wait_recv()
                flight.wait_send()
            self.add(0, mine, [self.from_ctx.at[step]])
        done = self.whole.at[self.span(0, self.core), mine]
        self.results = [self.links.local(done, self.final.at[:, mine])]
        if self.pair is not None:
            flight = self.links.send(
                done, self.other, flip(self.ctx, self.pair), self.wsh_of(0, self.core)
            )
            yield
            flight.wait_recv()
            self.results.append(self.links.local(self.other, self.final.at[:, self.side(False)]))
        yield


class TableSum:
    def __init__(self, links, table, slots, place, zs, ctxs):
        self.links, self.table, self.slots = links, table, slots
        ctx, z, core = place
        self.hops = (
            [[(ctx, z * 2 + 1 - core)]]
            + [[(ctx, flip(z, o) * 2 + core) for o in range(1, zs)]]
            + [[(flip(ctx, b), z * 2 + core)] for b in bits_of(ctxs)]
        )

    def steps(self):
        slot = 0
        for peers in self.hops:
            flights = []
            for n, peer in enumerate(peers):
                flights.append(
                    self.links.send(self.table, self.slots.at[slot + n], *peer)
                )
            yield
            total = self.table[...]
            for n, flight in enumerate(flights):
                flight.wait_recv()
                flight.wait_send()
                total = total + self.slots[slot + n]
            self.table[...] = total
            slot += len(peers)
        yield


DOWN_SPLIT = 256
BACK_SPLIT = 512
PAIRS = (1, 2, 2, 1)
BACK_PAIRS = (1, 2, 2, None, 1)
PLAN = (
    ("t", "q0", "o0", "u0", "tx", "q1", "u1", "q2", "o1", "o2", "q3",),
    ("u2", "e0", "d0", "r", "o3",),
    ("u3", "c", "qp", "e1", "op", "qf",),
    ("of",),
    ("e2", "d1", "e3", "cx",),
    ("up", "ep", "d2", "uf",),
    ("d3", "P", "df", "rx", "ef",),
)
BACK = (
    ("l",),
    (),
    ("d", "e", "l",),
    (),
    (),
    ("e", "d",),
    (),
    ("u",),
    ("e",),
    (),
    (
        "e", "s", "u", "q", "q", "e", "d", "e", "o", "u", "e", "H", "g", "o", "o", "s", "u",
        "d", "q", "u", "q", "o", "u", "e", "u", "q", "g", "q", "e", "u", "o", "o", "o", "q",
        "s", "d", "q", "o", "s", "u", "q", "K", "o", "u", "e", "d", "s", "q", "o",
    ),
)


def layer_kernel(
    ctxs,
    zs,
    pairs,
    back_pairs,
    tok,
    cot,
    order,
    order_block,
    vec_0,
    vec_1,
    vec_2,
    vec_3,
    vec_4,
    vec_5,
    vec_6,
    vec_7,
    vec_8,
    qkv_shard,
    out_shard,
    up_shard,
    down_shard,
    home_out,
    home_grad,
    sum_qkv,
    sum_out,
    sum_up,
    sum_down,
    sum_768,
    sum_wide,
    all_tok,
    all_cot,
    all_out,
    all_grad,
    order_column,
    vectors,
    all_order,
    all_vectors,
    w_qkv,
    w_out,
    w_up,
    w_down,
    g_down,
    stage,
    acc,
    inputs,
    low,
    top,
    qkv,
    probs,
    context,
    turned,
    first_norm,
    first_factor,
    hidden,
    slope,
    grad_wide,
    grad_low,
    result_low,
    back_low,
    rows_768,
    row_up,
    small,
    small_slots,
    *rest,
):
    buffers = [rest[5 * n : 5 * n + 5] for n in range(5)]
    send_sem, recv_sem = rest[25:27]
    vec_parts = rest[27:]
    back_split = BACK_SPLIT
    rows, width = tok.shape
    wide = up_shard.shape[1]
    pairs_of_heads = width // LANES
    blocks = rows // CLUSTER
    scale = HEAD_DIM**-0.5
    ctx = lax.axis_index("ctx")
    wsh = lax.axis_index("wsh")
    z, core = wsh // 2, wsh % 2
    place = (ctx, z, core)
    links = Links(send_sem, recv_sem)

    brought = [
        links.local(vector, vec_parts[n])
        for n, vector in enumerate(
            (vec_0, vec_1, vec_2, vec_3, vec_4, vec_5, vec_6, vec_7, vec_8)
        )
    ]
    vectors[...] = jnp.zeros_like(vectors)
    for n, copy in enumerate(brought):
        copy.wait()
        vectors[n : n + 1, 0 : vec_parts[n].shape[0]] = vec_parts[n][...].reshape(1, -1)
    order_column[...] = (
        jnp.broadcast_to(order[...].astype(f32), (LANES, rows)).T.astype(jnp.int32)
    )

    barrier = pltpu.get_barrier_semaphore()
    stream_peers = [
        (ctx, flip(z, o) * 2 + (core if same else 1 - core))
        for o in range(zs)
        for same in (True, False)
        if o > 0 or not same
    ]
    peers = stream_peers + [(flip(ctx, b), wsh) for b in bits_of(ctxs)]
    for peer in peers:
        pl.semaphore_signal(barrier, 1, device_id=peer, device_id_type=pl.DeviceIdType.MESH)
    pl.semaphore_wait(barrier, len(peers))

    tok_gather = CtxGather(links, tok, all_tok, ctx, wsh, ctxs, 2)
    cot_gather = CtxGather(links, cot, all_cot, ctx, wsh, ctxs, 2)
    order_gather = CtxGather(links, order_block, all_order, ctx, wsh, ctxs, 1)
    vec_own = links.local(vectors, all_vectors.at[wsh])
    vec_flights = [links.send(vectors, all_vectors.at[wsh], *peer) for peer in stream_peers]
    split = DOWN_SPLIT
    parts = [
        (qkv_shard, w_qkv, pairs[0]),
        (out_shard, w_out, pairs[1]),
        (up_shard, w_up, pairs[2]),
        (down_shard.at[:, pl.ds(0, split)], w_down.at[:, pl.ds(0, split)], pairs[3]),
        (
            down_shard.at[:, pl.ds(split, width - split)],
            w_down.at[:, pl.ds(split, width - split)],
            None,
        ),
    ]
    weights = dict(
        zip("quoed", [WeightGather(links, *parts[n], place, zs) for n in (0, 2, 1, 3, 4)])
    )
    rows_in = {"t": tok_gather, "r": order_gather, "c": cot_gather}

    def act(plan):
        for step in plan:
            if step == "P":
                pick(cot_gather, cot, acc)
                row_pass(CLUSTER, keep_top)
                continue
            if step[0] in rows_in:
                gather = rows_in[step[0]]
                if gather.step < gather.steps:
                    gather.advance()
                while step[1:] == "x" and gather.step < gather.steps:
                    gather.advance()
                continue
            gather, kind = weights[step[0]], step[1]
            if kind == "0":
                gather.start()
            elif kind == "3":
                for hop in range(3, zs):
                    gather.hop(hop)
            elif kind in "12":
                gather.hop(int(kind))
            elif kind == "p":
                gather.take_pair()
            else:
                gather.finish()

    act(PLAN[0])
    vec_own.wait()
    for flight in vec_flights:
        flight.wait_recv()

    rows_768[...] = jnp.zeros_like(rows_768)
    row_up[...] = jnp.zeros_like(row_up)
    length = width // (2 * zs)

    def spread(part, spot, size, target):
        first = min(spot // LANES * LANES, target.shape[1] - 2 * part.shape[1])
        shape = (part.shape[1], 2 * part.shape[1])
        j = lax.broadcasted_iota(jnp.int32, shape, 0)
        col = lax.broadcasted_iota(jnp.int32, shape, 1)
        move = jnp.where((col == j + (spot - first)) & (j < size), 1.0, 0.0).astype(bf16)
        at = pl.ds(first, shape[1])
        target[:, at] = target[:, at] + mm(part, move)[: target.shape[0]]

    length_up = wide // (2 * zs)
    for s in range(2 * zs):
        spread(all_vectors[s, :, 0:LANES], length * s, length, rows_768)
        if length_up % LANES == 0:
            up_part = all_vectors[s, 8:16, 0:length_up].astype(f32)
            row_up[0:1, length_up * s : length_up * (s + 1)] = up_part[0:1]
        else:
            spread(all_vectors[s, 8:16, :], length_up * s, length_up, row_up)

    def keep_top(here):
        top[here, :] = acc[here, :].astype(bf16)

    def pick(gather, own, total):
        copies = {}

        def fetch(offset):
            if offset == 0:
                src = own
            else:
                gather.need(offset)
                src = gather.buffer.at[flip(ctx, offset)]
            copies[offset] = links.local(src, stage.at[offset % 2])

        fetch(0)
        for offset in range(ctxs):
            copies[offset].wait()
            if offset + 1 < ctxs:
                fetch(offset + 1)
            first = flip(ctx, offset) * rows

            def body(i, carry):
                here = pl.ds(pl.multiple_of(i * CLUSTER, CLUSTER), CLUSTER)
                place_of = order_column[here, :]
                lane = lax.broadcasted_iota(jnp.int32, (CLUSTER, LANES), 1)
                chosen = jnp.concatenate(
                    [
                        jnp.where(place_of == lane + (first + t * LANES), 1.0, 0.0).astype(bf16)
                        for t in range(rows // LANES)
                    ],
                    axis=1,
                )
                got = mm(chosen, stage[offset % 2])
                total[here, :] = got if offset == 0 else total[here, :] + got
                return carry

            lax.fori_loop(0, blocks, body, 0)

    def bring_home(gather, own, target):
        copies = {}

        def fetch(offset):
            if offset == 0:
                src = own
            else:
                gather.need(offset)
                src = gather.buffer.at[flip(ctx, offset)]
            copies[offset] = links.local(src, stage.at[offset % 2])

        fetch(0)
        for offset in range(ctxs):
            copies[offset].wait()
            if offset + 1 < ctxs:
                fetch(offset + 1)
            if offset == 0:
                places = order[...]
            else:
                order_gather.need(offset)
                places = all_order[flip(ctx, offset)]

            def body(i, carry):
                here = pl.ds(pl.multiple_of(i * CLUSTER, CLUSTER), CLUSTER)
                token = lax.broadcasted_iota(jnp.int32, (CLUSTER, rows), 0) + (
                    ctx * rows + i * CLUSTER
                )
                chosen = jnp.where(places[0:1, :] == token, 1.0, 0.0).astype(bf16)
                got = mm(chosen, stage[offset % 2])
                if offset > 0:
                    got = acc[here, :] + got
                if offset == ctxs - 1:
                    target[here, :] = got.astype(bf16)
                else:
                    acc[here, :] = got
                return carry

            lax.fori_loop(0, blocks, body, 0)

    def tiles(columns, body, first=0):
        def step(t, carry):
            body(t, pl.ds(pl.multiple_of(t * STEP, STEP), STEP))
            return carry

        lax.fori_loop(first // STEP, columns // STEP, step, 0)

    def row_pass(size, body):
        def step(i, carry):
            body(pl.ds(pl.multiple_of(i * size, size), size))
            return carry

        lax.fori_loop(0, rows // size, step, 0)

    def tally(vector, values):
        total = jnp.sum(values, axis=0, keepdims=True)
        for t in range(width // STEP):
            at = pl.ds(vector * (width // STEP) + t, 1)
            small[at, :] = small[at, :] + total[:, t * STEP : (t + 1) * STEP]

    small[...] = jnp.zeros_like(small)
    qbias, vbias, obias, gain1, shift1, dbias, gain2, shift2 = [
        rows_768.at[pl.ds(n, 1)] for n in range(8)
    ]

    act(PLAN[1])
    pick(tok_gather, tok, acc)

    def keep_inputs(here):
        inputs[here, :] = acc[here, :].astype(bf16)

    row_pass(CLUSTER, keep_inputs)
    act(PLAN[2])

    def project(t, span):
        at = pl.ds(pl.multiple_of((t % (width // STEP)) * STEP, STEP), STEP)
        part = t // (width // STEP)
        bias = jnp.where(part == 0, qbias[:, at], jnp.where(part == 2, vbias[:, at], 0.0))
        qkv[:, span] = (mm(inputs[...], w_qkv[:, span]) + bias).astype(bf16)

    tiles(3 * width, project)

    act(PLAN[3])

    lane = lax.broadcasted_iota(jnp.int32, (1, LANES), 1)
    left = jnp.where(lane < HEAD_DIM, 1.0, 0.0).astype(bf16)
    right = jnp.where(lane < HEAD_DIM, 0.0, 1.0).astype(bf16)

    def both(values):
        return jnp.concatenate([values * left, values * right], axis=0)

    def side_by_side(values):
        return jnp.concatenate([values[:CLUSTER], values[CLUSTER:]], axis=1)

    def part_of(here, kind, pair):
        return qkv[here, kind * width + pair * LANES : kind * width + (pair + 1) * LANES]

    def attend(b, carry):
        here = pl.ds(pl.multiple_of(b * CLUSTER, CLUSTER), CLUSTER)
        visible = order[0:1, here] <= order_column[here, :]
        hide = jnp.where(visible, 0.0, -1e30)
        hide = jnp.concatenate([hide, hide], axis=0)
        for pair in range(pairs_of_heads):
            query, keyed, valued = [part_of(here, kind, pair) for kind in range(3)]
            scores = mm_nt(both(query), keyed) * scale + hide
            expd = jnp.exp(scores - jnp.max(scores, axis=1, keepdims=True))
            prob = expd * (1.0 / jnp.sum(expd, axis=1, keepdims=True))
            probs[b * pairs_of_heads + pair] = prob
            got = mm(side_by_side(prob.astype(bf16)), both(valued))
            context[here, pair * LANES : (pair + 1) * LANES] = got.astype(bf16)
        return carry

    lax.fori_loop(0, blocks, attend, 0)
    act(PLAN[4])

    def out_project(t, span):
        acc[:, span] = mm(context[...], w_out[:, span])

    tiles(width, out_project)

    def first_normalize(here):
        attended = (acc[here, :] + obias[...]).astype(bf16).astype(f32)
        resid = inputs[here, :].astype(f32) + attended
        centre = resid - jnp.mean(resid, axis=1, keepdims=True)
        factor = lax.rsqrt(jnp.mean(centre * centre, axis=1, keepdims=True) + epsilon)
        normed = centre * factor
        first_norm[here, :] = normed
        first_factor[here, :] = factor
        low[here, :] = (normed * gain1[...] + shift1[...]).astype(bf16)

    row_pass(64, first_normalize)
    act(PLAN[5])

    def feed(t, span):
        pre = mm(low[...], w_up[:, span]) + row_up[0:1, span]
        half = 0.5 * (1.0 + lax.erf(pre * 0.7071067811865476))
        hidden[:, span] = (pre * half).astype(bf16)
        slope[:, span] = (half + pre * jnp.exp(-0.5 * pre * pre) * 0.3989422804014327).astype(bf16)

    tiles(wide, feed)
    act(PLAN[6])

    def down(t, span):
        acc[:, span] = mm(hidden[...], w_down[:, span])

    tiles(width, down)

    def second_normalize(here):
        first_out = first_norm[here, :] * gain1[...] + shift1[...]
        second_in = first_out + acc[here, :] + dbias[...]
        centre = second_in - jnp.mean(second_in, axis=1, keepdims=True)
        factor = lax.rsqrt(jnp.mean(centre * centre, axis=1, keepdims=True) + epsilon)
        normed = centre * factor
        result_low[here, :] = (normed * gain2[...] + shift2[...]).astype(bf16)
        grad_top = top[here, :].astype(f32)
        tally(6, grad_top * normed)
        tally(7, grad_top)
        grad_normed = grad_top * gain2[...]
        grad = factor * (
            grad_normed
            - jnp.mean(grad_normed, axis=1, keepdims=True)
            - normed * jnp.mean(grad_normed * normed, axis=1, keepdims=True)
        )
        grad_wide[here, :] = grad
        grad = grad.astype(bf16)
        grad_low[here, :] = grad
        tally(5, grad.astype(f32))

    row_pass(64, second_normalize)

    scatters = [
        GradScatter(links, w, f, b, place, zs, ctxs, p)
        for w, f, b, p in zip(
            (
                w_qkv,
                w_out,
                w_up,
                g_down.at[:, pl.ds(0, back_split)],
                g_down.at[:, pl.ds(back_split, width - back_split)],
            ),
            (
                sum_qkv,
                sum_out,
                sum_up,
                sum_down.at[:, pl.ds(0, back_split)],
                sum_down.at[:, pl.ds(back_split, width - back_split)],
            ),
            buffers,
            back_pairs,
        )
    ]
    gathered, links.sent = links.sent, []
    out_gather = CtxGather(links, result_low, all_out, ctx, wsh, ctxs, 2)
    back = {}

    def go(plan):
        for step in plan:
            if step in back:
                next(back[step], None)

    def through(gather):
        while gather.step < gather.steps:
            gather.advance()
            yield

    def at_home(gather, own, target):
        for _ in through(gather):
            pass
        bring_home(gather, own, target)
        yield

    back["l"] = through(out_gather)
    go(BACK[0])
    part_rows = wide // (2 * zs)

    def down_grad(owner):
        def body(i, carry):
            here = pl.ds(pl.multiple_of((i * 2 + owner) * part_rows, LANES // 2), part_rows)
            turned_hidden = hidden_turned(i * 2 + owner)
            g_down[here, :] = mm(turned_hidden, grad_low[...]).astype(bf16)
            return carry

        lax.fori_loop(0, zs, body, 0)

    if part_rows % LANES == 0:

        def hidden_turned(s):
            return hidden[:, pl.ds(pl.multiple_of(s * part_rows, LANES), part_rows)].T

        down_grad(1 - core)
        scatters[3].send_core()
        scatters[4].send_core()
        down_grad(core)
    else:

        def all_down(t, span):
            g_down[span, :] = mm(hidden[:, span].T, grad_low[...]).astype(bf16)

        tiles(wide, all_down)
        scatters[3].send_core()
        scatters[4].send_core()

    def back_hidden(t, span):
        grad = (mm_nt(grad_low[...], w_down[span, :]) * slope[:, span]).astype(bf16)
        slope[:, span] = grad
        small[pl.ds(8 * (width // STEP) + t, 1), :] = jnp.sum(
            grad.astype(f32), axis=0, keepdims=True
        )

    tiles(wide // 2, back_hidden)
    back["d"] = scatters[3].steps()
    back["e"] = scatters[4].steps()
    go(BACK[1])
    tiles(wide, back_hidden, wide // 2)
    go(BACK[2])

    def back_up(t, span):
        acc[:, span] = mm_nt(slope[...], w_up[span, :])

    tiles(width, back_up)

    def first_back(here):
        grad_first = grad_wide[here, :] + acc[here, :]
        normed = first_norm[here, :]
        tally(3, grad_first * normed)
        tally(4, grad_first)
        grad_normed = grad_first * gain1[...]
        grad = first_factor[here, :] * (
            grad_normed
            - jnp.mean(grad_normed, axis=1, keepdims=True)
            - normed * jnp.mean(grad_normed * normed, axis=1, keepdims=True)
        )
        grad_wide[here, :] = grad
        grad = grad.astype(bf16)
        grad_low[here, :] = grad
        tally(2, grad.astype(f32))

    row_pass(64, first_back)
    go(BACK[3])
    for flight in gathered:
        flight.wait_send()

    turned[...] = low[...].T

    def up_grad(t, span):
        w_up[:, span] = mm(turned[...], slope[:, span]).astype(bf16)

    tiles(wide, up_grad)
    scatters[2].send_core()
    back["u"] = scatters[2].steps()

    turned[...] = context[...].T

    def back_context(t, span):
        context[:, span] = mm_nt(grad_low[...], w_out[span, :]).astype(bf16)

    tiles(width, back_context)

    def out_grad(t, span):
        w_out[:, span] = mm(turned[...], grad_low[:, span]).astype(bf16)

    tiles(width, out_grad)
    scatters[1].send_core()
    back["o"] = scatters[1].steps()
    go(BACK[4])

    def back_attend(b, carry):
        here = pl.ds(pl.multiple_of(b * CLUSTER, CLUSTER), CLUSTER)
        for pair in range(pairs_of_heads):
            query, keyed, valued = [part_of(here, kind, pair) for kind in range(3)]
            prob = probs[b * pairs_of_heads + pair]
            grad = both(context[here, pair * LANES : (pair + 1) * LANES])
            grad_prob = mm_nt(grad, valued)
            grad_valued = mm_tn(prob.astype(bf16), grad)
            inner = jnp.sum(prob * grad_prob, axis=1, keepdims=True)
            grad_score = (prob * (grad_prob - inner)).astype(bf16)
            grad_query = mm(side_by_side(grad_score), both(keyed)) * scale
            grad_keyed = mm_tn(grad_score, both(query)) * scale
            for kind, value in enumerate((grad_query, grad_keyed, grad_valued)):
                at = kind * width + pair * LANES
                qkv[here, at : at + LANES] = value.astype(bf16)
        return carry

    for b in range(blocks):
        lax.fori_loop(b, b + 1, back_attend, 0)
        go(BACK[5 + min(b, 3)])

    def input_sums(here):
        tally(0, qkv[here, 0:width].astype(f32))
        tally(1, qkv[here, 2 * width : 3 * width].astype(f32))

    row_pass(64, input_sums)

    def back_qkv(t, span):
        back_low[:, span] = (mm_nt(qkv[...], w_qkv[span, :]) + grad_wide[:, span]).astype(bf16)

    table = TableSum(links, small, small_slots, place, zs, ctxs)
    back["s"] = table.steps()
    tiles(width, back_qkv)
    go(BACK[9])
    grad_gather = CtxGather(links, back_low, all_grad, ctx, wsh, ctxs, 2)
    turned[...] = inputs[...].T

    def qkv_grad(t, span):
        w_qkv[:, span] = mm(turned[...], qkv[:, span]).astype(bf16)

    tiles(3 * width, qkv_grad)
    scatters[0].send_core()
    back["q"] = scatters[0].steps()
    back["g"] = through(grad_gather)
    back["H"] = at_home(out_gather, result_low, home_out)
    back["K"] = at_home(grad_gather, back_low, home_grad)
    go(BACK[10])
    running = list(back.values())
    while running:
        running = [steps for steps in running if next(steps, "end") != "end"]
    count = width // STEP
    for n in range(8):
        for t in range(count):
            sum_768[n : n + 1, t * STEP : (t + 1) * STEP] = small[n * count + t : n * count + t + 1]
    for t in range(wide // STEP):
        sum_wide[0:1, t * STEP : (t + 1) * STEP] = small[8 * count + t : 8 * count + t + 1]
    links.drain()
    for scatter in scatters:
        for result in scatter.results:
            result.wait()


def finish_kernel(wshs, *refs):
    sources, (sum_768, sum_wide) = refs[:6], refs[6:8]
    targets, vecs = refs[8:14], refs[14:23]
    taken, given, sem = refs[23:29], refs[29:35], refs[35]
    coming = [pltpu.make_async_copy(s, t, sem.at[n]) for n, (s, t) in enumerate(zip(sources, taken))]
    for copy in coming:
        copy.start()
    me = lax.axis_index("wsh")
    for sums, outs in ((sum_768, vecs[:8]), (sum_wide, vecs[8:])):
        size = outs[0].shape[0]
        columns = sums.shape[1]
        mine = pltpu.roll(sums[...], lax.rem(columns - me * size, columns), 1)
        for n, out in enumerate(outs):
            out[...] = mine[n, 0:size]
    going = []
    for n, copy in enumerate(coming):
        copy.wait()
        given[n][...] = taken[n][...].astype(given[n].dtype)
        going.append(pltpu.make_async_copy(given[n], targets[n], sem.at[6 + n]))
        going[-1].start()
    for copy in going:
        copy.wait()


def on_device(
    ctxs,
    wshs,
    tokens,
    cluster_order,
    qkv_weight,
    query_bias,
    value_bias,
    out_weight,
    out_bias,
    first_gain,
    first_shift,
    up_weight,
    up_bias,
    down_weight,
    down_bias,
    second_gain,
    second_shift,
    cotangent,
):
    rows, width = tokens.shape[1:]
    wide = up_weight.shape[1]
    zs = wshs // 2
    small_rows = 8 * (width // STEP) + wide // STEP
    small_rows = (small_rows + 7) // 8 * 8
    vector_lanes = (up_bias.shape[0] + LANES - 1) // LANES * LANES
    heads_pairs = width // LANES
    blocks = rows // CLUSTER
    hops = zs + len(bits_of(ctxs))
    shards = [qkv_weight.shape, out_weight.shape, up_weight.shape, down_weight.shape]
    sems = 2 * wshs + 4 * 2 * ctxs * 2 + 10 * zs * 4 + 4 * (4 * zs + 8) + 64

    def vmem(shape, dtype=bf16):
        return pltpu.VMEM(shape, dtype)

    pairs, back_pairs = PAIRS, BACK_PAIRS
    landing = []
    rows_down = down_weight.shape[0]
    pieces = shards[:3] + [(rows_down, BACK_SPLIT), (rows_down, width - BACK_SPLIT)]
    for (n, columns), pair in zip(pieces, back_pairs):
        part = columns // 2
        landing.append(vmem((zs, n, columns)))
        if pair is None:
            landing.append(vmem((1, 16, LANES)))
            landing.append(vmem((zs - 1, n, columns)))
            landing.append(vmem((len(bits_of(ctxs)), n, columns)))
            landing.append(vmem((16, LANES)))
        else:
            landing.append(vmem((zs, n, part)))
            landing.append(vmem((zs - 1, n, part)))
            landing.append(vmem((len(bits_of(ctxs)) - 1, n, part)))
            landing.append(vmem((n, part)))
    anywhere = pl.BlockSpec(memory_space=pl.ANY)
    on_chip = pl.BlockSpec(memory_space=pltpu.VMEM)
    many = jax.ShapeDtypeStruct((ctxs, rows, width), bf16)
    results = pl.pallas_call(
        functools.partial(layer_kernel, ctxs, zs, pairs, back_pairs),
        out_shape=[
            jax.ShapeDtypeStruct((rows, width), bf16),
            jax.ShapeDtypeStruct((rows, width), bf16),
        ]
        + [jax.ShapeDtypeStruct(s, bf16) for s in shards]
        + [jax.ShapeDtypeStruct((8, width), f32), jax.ShapeDtypeStruct((8, wide), f32)]
        + [many] * 4,
        in_specs=[anywhere, anywhere, on_chip, anywhere] + [anywhere] * 13,
        out_specs=[on_chip, on_chip] + [anywhere] * 4 + [on_chip] * 2 + [anywhere] * 4,
        scratch_shapes=[
            vmem((rows, LANES), jnp.int32),
            vmem((16, vector_lanes)),
            vmem((ctxs, 1, rows), jnp.int32),
            vmem((wshs, 16, vector_lanes)),
            vmem((width, 3 * width)),
            vmem((width, width)),
            vmem((width, wide)),
            vmem((wide, width)),
            vmem((wide, width)),
            vmem((2, rows, width)),
            vmem((rows, width), f32),
            vmem((rows, width)),
            vmem((rows, width)),
            vmem((rows, width)),
            vmem((rows, 3 * width)),
            vmem((blocks * heads_pairs, 2 * CLUSTER, CLUSTER), f32),
            vmem((rows, width)),
            vmem((width, rows)),
            vmem((rows, width), f32),
            vmem((rows, 1), f32),
            vmem((rows, wide)),
            vmem((rows, wide)),
            vmem((rows, width), f32),
            vmem((rows, width)),
            vmem((rows, width)),
            vmem((rows, width)),
            vmem((8, width), f32),
            vmem((8, wide), f32),
            vmem((small_rows, STEP), f32),
            vmem((hops, small_rows, STEP), f32),
        ]
        + landing
        + [pltpu.SemaphoreType.DMA((sems,)), pltpu.SemaphoreType.DMA((sems,))]
        + [vmem(query_bias.shape)] * 8
        + [vmem(up_bias.shape)],
        compiler_params=pltpu.CompilerParams(
            collective_id=0, has_side_effects=True, vmem_limit_bytes=67043328
        ),
        name="layer",
    )(
        tokens[0],
        cotangent[0],
        cluster_order,
        cluster_order,
        query_bias,
        value_bias,
        out_bias,
        first_gain,
        first_shift,
        down_bias,
        second_gain,
        second_shift,
        up_bias,
        qkv_weight,
        out_weight,
        up_weight,
        down_weight,
    )
    big = results[:6]
    part = width // wshs
    part_wide = wide // wshs
    outs = [jax.ShapeDtypeStruct((rows, width), bf16), jax.ShapeDtypeStruct((rows, width), f32)]
    outs += [jax.ShapeDtypeStruct(s, f32) for s in shards]
    outs += [jax.ShapeDtypeStruct((part,), f32)] * 8 + [jax.ShapeDtypeStruct((part_wide,), f32)]
    (home_out, home_grad, g_qkv, g_out, g_up, g_down, *vecs) = pl.pallas_call(
        functools.partial(finish_kernel, wshs),
        out_shape=outs,
        in_specs=[anywhere] * 6 + [on_chip] * 2,
        out_specs=[anywhere] * 6 + [on_chip] * 9,
        scratch_shapes=[vmem(v.shape) for v in big]
        + [vmem(v.shape, o.dtype) for v, o in zip(big, outs)]
        + [pltpu.SemaphoreType.DMA((12,))],
        compiler_params=pltpu.CompilerParams(vmem_limit_bytes=67043328),
        name="finish",
    )(*big, *results[6:8])
    g_q, g_v, g_o, g_g1, g_s1, g_d, g_g2, g_s2, g_u = vecs
    return (
        home_out[None],
        home_grad[None],
        g_qkv,
        g_q,
        g_v,
        g_out,
        g_o,
        g_g1,
        g_s1,
        g_up,
        g_u,
        g_down,
        g_d,
        g_g2,
        g_s2,
    )


def solution(mesh):
    row = P("wsh", None)
    vec = P("wsh")
    seq = P("wsh", "ctx", None)
    in_specs = (
        seq,
        P("wsh", "ctx"),
        row,
        vec,
        vec,
        row,
        vec,
        vec,
        vec,
        row,
        vec,
        row,
        vec,
        vec,
        vec,
        seq,
    )
    out_specs = (
        seq,
        seq,
        row,
        vec,
        vec,
        row,
        vec,
        vec,
        vec,
        row,
        vec,
        row,
        vec,
        vec,
        vec,
    )
    return jax.shard_map(
        functools.partial(on_device, mesh.shape["ctx"], mesh.shape["wsh"]),
        mesh=mesh,
        in_specs=in_specs,
        out_specs=out_specs,
        check_vma=False,
    )
```

```python
import functools

import jax
import jax.numpy as jnp
from jax import lax
from jax.experimental import pallas as pl
from jax.experimental.pallas import tpu as pltpu
from jax.sharding import PartitionSpec as P

HEAD_DIM = 64
CLUSTER = 128
LANES = 128
STEP = 256

epsilon = 1e-05
bf16 = jnp.bfloat16
f32 = jnp.float32


def mm(left, right):
    return lax.dot_general(left, right, (((1,), (0,)), ((), ())), preferred_element_type=f32)


def mm_nt(left, right):
    return lax.dot_general(left, right, (((1,), (1,)), ((), ())), preferred_element_type=f32)


def mm_tn(left, right):
    return lax.dot_general(left, right, (((0,), (0,)), ((), ())), preferred_element_type=f32)


def flip(index, offset):
    bit = 1
    result = index
    while bit <= offset:
        if offset & bit:
            result = result + bit * (1 - 2 * ((index // bit) % 2))
        bit *= 2
    return result


def bits_of(size):
    found, bit = [], 1
    while bit < size:
        found.append(bit)
        bit *= 2
    return found


def low_bit(value):
    return value & -value


def only_if(condition, action):
    if condition is None:
        action()
    else:
        pl.when(condition)(action)


class Flight:
    def __init__(self, copy, landing=None, sends=None, receives=None):
        self.copy, self.landing = copy, landing or copy
        self.sends, self.receives = sends, receives
        self.leaving = self.coming = True
        only_if(sends, copy.start)

    def wait_recv(self):
        if self.coming:
            only_if(self.receives, self.landing.wait_recv)
        self.coming = False

    def wait_send(self):
        if self.leaving:
            only_if(self.sends, self.copy.wait_send)
        self.leaving = False


class Links:
    def __init__(self, send_sem, recv_sem):
        self.send_sem, self.recv_sem, self.used = send_sem, recv_sem, 0
        self.sent = []

    def remote(self, n, src, dst, ctx, wsh):
        return pltpu.make_async_remote_copy(
            src_ref=src,
            dst_ref=dst,
            send_sem=self.send_sem.at[n],
            recv_sem=self.recv_sem.at[n],
            device_id=(ctx, wsh),
            device_id_type=pl.DeviceIdType.MESH,
        )

    def send(self, src, dst, ctx, wsh, landing=None, sends=None, receives=None):
        n = self.used
        self.used += 1
        if landing is not None:
            landing = self.remote(n, landing, landing, ctx, wsh)
        flight = Flight(self.remote(n, src, dst, ctx, wsh), landing, sends, receives)
        self.sent.append(flight)
        return flight

    def local(self, src, dst):
        n = self.used
        self.used += 1
        copy = pltpu.make_async_copy(src, dst, self.send_sem.at[n])
        copy.start()
        return copy

    def drain(self):
        for flight in self.sent:
            flight.wait_send()
        self.sent = []


class CtxGather:
    def __init__(self, links, own, buffer, ctx, wsh, count, halves):
        self.links, self.own, self.buffer, self.ctx, self.wsh = links, own, buffer, ctx, wsh
        rows = buffer.shape[1] // halves
        self.spans = [pl.ds(h * rows, rows) for h in range(halves)]
        order = bits_of(count)
        self.orders = [order, order[1::-1] + order[2:]][:halves]
        self.have = [{0: None} for _ in self.spans]
        self.step = 0
        self.steps = len(order)

    def advance(self):
        for h, span in enumerate(self.spans):
            bit = self.orders[h][self.step]
            new = {}
            for offset, arrival in self.have[h].items():
                if arrival is not None:
                    arrival.wait_recv()
                    self.have[h][offset] = None
                block = flip(self.ctx, offset)
                src = self.own.at[span] if offset == 0 else self.buffer.at[block, span]
                new[offset ^ bit] = self.links.send(
                    src, self.buffer.at[block, span], flip(self.ctx, bit), self.wsh
                )
            self.have[h].update(new)
        self.step += 1

    def need(self, offset):
        for have in self.have:
            if have[offset] is not None:
                have[offset].wait_recv()
                have[offset] = None


class RowRoute:
    def __init__(self, links, buffer, place, count, cap, shared):
        self.links, self.buffer = links, buffer
        self.ctx, self.wsh = place
        self.count, self.cap = count, cap
        self.rows_out, self.landed, self.using = shared
        self.kept, self.flights, self.passing = {}, {}, {}

    def block(self, of):
        return pl.ds(pl.multiple_of(of * self.cap, 16), self.cap)

    def free(self, phase):
        for flight in self.using.pop(phase, []):
            flight.wait_send()

    def send(self, phase):
        flights = {}
        leaving = []
        slot = phase * self.count
        for offset in sorted(range(1, self.count), reverse=self.count == 4):
            to = flip(self.ctx, offset)
            rows = self.rows_out.at[phase, self.block(to)]
            if self.count == 4 and offset == 3:
                passing = self.links.send(
                    rows, self.buffer.at[2 * self.count + phase], flip(self.ctx, 1), self.wsh
                )
                self.passing[phase] = passing
                leaving.append(passing)
                continue
            flights[offset] = self.links.send(
                rows,
                self.buffer.at[slot + self.ctx],
                to,
                self.wsh,
                landing=self.buffer.at[slot + to],
            )
        self.flights[phase] = flights
        kept = Kept(
            self.links.local(
                self.rows_out.at[phase, self.block(self.ctx)], self.buffer.at[slot + self.ctx]
            )
        )
        self.kept[phase] = kept
        self.using[phase] = leaving + list(flights.values()) + [kept]

    def forward(self, phase):
        if self.count == 4:
            self.passing[phase].wait_recv()
            slot = phase * self.count
            self.flights[phase][3] = self.links.send(
                self.buffer.at[2 * self.count + phase],
                self.buffer.at[slot + flip(self.ctx, 1)],
                flip(self.ctx, 2),
                self.wsh,
                landing=self.buffer.at[slot + flip(self.ctx, 3)],
            )

    def collect(self, phase):
        self.kept[phase].wait_send()
        copies = []
        for offset in range(self.count):
            if offset > 0:
                self.flights[phase][offset].wait_recv()
            of = flip(self.ctx, offset)
            copies.append(
                self.links.local(
                    self.buffer.at[phase * self.count + of], self.landed.at[self.block(of)]
                )
            )
        for copy in copies:
            copy.wait()


class Kept:
    def __init__(self, copy):
        self.copy, self.leaving = copy, True

    def wait_send(self):
        if self.leaving:
            self.copy.wait()
        self.leaving = False


class WeightGather:
    def __init__(self, links, shard, whole, pair, place, zs):
        self.links, self.shard, self.whole = links, shard, whole
        self.ctx, self.z, self.core = place
        self.zs, self.pair = zs, pair
        self.rows, self.columns = shard.shape
        self.moving, self.from_pair, self.from_core = {}, [], []

    def row_span(self, z, core):
        return pl.ds(pl.multiple_of((z * 2 + core) * self.rows, 16), self.rows)

    def side(self, mine):
        if self.pair is None:
            return pl.ds(0, self.columns)
        half = self.columns // 2
        side = (self.ctx // self.pair) % 2
        if not mine:
            side = 1 - side
        return pl.ds(pl.multiple_of(side * half, LANES), half)

    def away(self, way, hop):
        return (self.z - way * hop + 2 * self.zs) % self.zs

    def arrives(self, way, hop):
        return self.z >= hop if way > 0 else self.z + hop < self.zs

    def can_send(self, way):
        return self.z + 1 < self.zs if way > 0 else self.z > 0

    def forward(self, way, hop, src):
        mine = self.side(True)
        here = self.away(way, hop)
        sends = self.can_send(way)
        if hop > 0:
            sends = jnp.logical_and(sends, self.arrives(way, hop))
        self.moving[way, hop + 1] = self.links.send(
            src,
            self.whole.at[self.row_span(here, self.core), mine],
            self.ctx,
            self.away(way, -1) * 2 + self.core,
            landing=self.whole.at[self.row_span(self.away(way, hop + 1), self.core), mine],
            sends=sends,
            receives=self.arrives(way, hop + 1),
        )

    def start(self):
        rows = self.row_span(self.z, self.core)
        for way in (1, -1):
            self.forward(way, 0, self.shard.at[:, self.side(True)])
        self.from_core.append(
            self.links.send(
                self.shard, self.whole.at[rows], self.ctx, self.z * 2 + 1 - self.core
            )
        )
        self.own = self.links.local(self.shard, self.whole.at[rows])

    def to_core(self, z, span, condition):
        part = self.whole.at[self.row_span(z, self.core), span]
        back = self.whole.at[self.row_span(z, 1 - self.core), span]
        self.from_core.append(
            self.links.send(
                part,
                part,
                self.ctx,
                self.z * 2 + 1 - self.core,
                landing=back,
                sends=condition,
                receives=condition,
            )
        )

    def hop(self, hop):
        mine = self.side(True)
        for way in (1, -1):
            self.moving.pop((way, hop)).wait_recv()
            z = self.away(way, hop)
            part = self.whole.at[self.row_span(z, self.core), mine]
            condition = self.arrives(way, hop)
            if hop + 1 < self.zs:
                self.forward(way, hop, part)
            if self.pair is not None:
                flight = self.links.send(
                    part,
                    part,
                    flip(self.ctx, self.pair),
                    self.z * 2 + self.core,
                    landing=self.whole.at[self.row_span(z, self.core), self.side(False)],
                    sends=condition,
                    receives=condition,
                )
                self.from_pair.append((z, condition, flight))
            self.to_core(z, mine, condition)

    def take_pair(self):
        for z, condition, flight in self.from_pair:
            flight.wait_recv()
            self.to_core(z, self.side(False), condition)
        self.from_pair = []

    def finish(self):
        self.own.wait()
        for flight in self.from_core:
            flight.wait_recv()


class GradScatter:
    def __init__(self, links, whole, final, buffers, place, zs, ctxs, pair):
        self.links, self.whole, self.final = links, whole, final
        self.from_core, self.from_pair, self.from_z, self.from_ctx, self.other = buffers
        self.ctx, self.z, self.core = place
        self.zs, self.pair = zs, pair
        self.rows, self.columns = whole.shape[0] // (2 * zs), whole.shape[1]
        self.cbits = [b for b in bits_of(ctxs) if b != pair]
        self.order = sorted(range(zs), key=lambda o: (-(o % 2), -o))

    def span(self, offset, core):
        first = (flip(self.z, offset) * 2 + core) * self.rows
        return pl.ds(pl.multiple_of(first, 16), self.rows)

    def side(self, mine):
        if self.pair is None:
            return pl.ds(0, self.columns)
        half = self.columns // 2
        side = (self.ctx // self.pair) % 2
        if not mine:
            side = 1 - side
        return pl.ds(pl.multiple_of(side * half, LANES), half)

    def wsh_of(self, offset, core):
        return flip(self.z, offset) * 2 + core

    def send_core(self):
        self.flights = []
        for offset in self.order:
            self.flights.append(
                self.links.send(
                    self.whole.at[self.span(offset, 1 - self.core)],
                    self.from_core.at[offset],
                    self.ctx,
                    self.wsh_of(0, 1 - self.core),
                )
            )

    def add(self, offset, columns, others):
        first = (flip(self.z, offset) * 2 + self.core) * self.rows
        piece = 48

        def body(i, carry):
            here = pl.ds(pl.multiple_of(first + i * piece, 16), piece)
            there = pl.ds(pl.multiple_of(i * piece, 16), piece)
            total = self.whole[here, columns].astype(f32)
            for other in others:
                total = total + other[there, :].astype(f32)
            self.whole[here, columns] = total.astype(bf16)
            return carry

        lax.fori_loop(0, self.rows // piece, body, 0)

    def send_pair(self, offset):
        columns = self.side(False)
        return self.links.send(
            self.whole.at[self.span(offset, self.core), columns],
            self.from_pair.at[offset],
            flip(self.ctx, self.pair),
            self.wsh_of(0, self.core),
        )

    def send_z(self, offset):
        columns = self.side(True)
        return self.links.send(
            self.whole.at[self.span(offset, self.core), columns],
            self.from_z.at[self.slot(low_bit(offset), offset - low_bit(offset))],
            self.ctx,
            self.wsh_of(low_bit(offset), self.core),
        )

    def slot(self, bit, offset):
        first = 0
        for earlier in bits_of(bit):
            first += self.zs // (2 * earlier)
        return first + offset // (2 * bit)

    def steps(self):
        mine = self.side(True)
        coming = {}
        in_pair = {}

        def pass_on(offset):
            if offset > 0:
                coming[offset - low_bit(offset)] = self.send_z(offset)

        for offset, flight in zip(self.order, self.flights):
            flight.wait_recv()
            self.add(offset, pl.ds(0, self.columns), [self.from_core.at[offset]])
            if self.pair is not None:
                in_pair[offset] = self.send_pair(offset)
            elif offset % 2:
                pass_on(offset)
        yield
        for offset, flight in in_pair.items():
            flight.wait_recv()
            self.add(offset, mine, [self.from_pair.at[offset]])
            if offset % 2:
                pass_on(offset)
            yield
        for bit in bits_of(self.zs):
            taken, coming = coming, {}
            for offset in sorted(taken, key=lambda o: -(o % (2 * bit) + (o & (2 * bit)))):
                taken[offset].wait_recv()
                self.add(offset, mine, [self.from_z.at[self.slot(bit, offset)]])
                if offset & (2 * bit):
                    pass_on(offset)
                if offset:
                    yield
            if 2 * bit < self.zs:
                yield
        half = self.columns // 2
        if self.pair is None:
            parts = [(pl.ds(0, half), self.cbits), (pl.ds(half, half), self.cbits[::-1])]
        else:
            parts = [(mine, self.cbits)]
        for step in range(len(self.cbits)):
            flights = []
            for columns, order in parts:
                there = columns if self.pair is None else pl.ds(0, half)
                flights.append(
                    self.links.send(
                        self.whole.at[self.span(0, self.core), columns],
                        self.from_ctx.at[step, :, there],
                        flip(self.ctx, order[step]),
                        self.wsh_of(0, self.core),
                    )
                )
            yield
            for flight in flights:
                flight.wait_recv()
                flight.wait_send()
            self.add(0, mine, [self.from_ctx.at[step]])
        done = self.whole.at[self.span(0, self.core), mine]
        self.results = [self.links.local(done, self.final.at[:, mine])]
        if self.pair is not None:
            flight = self.links.send(
                done, self.other, flip(self.ctx, self.pair), self.wsh_of(0, self.core)
            )
            yield
            flight.wait_recv()
            self.results.append(self.links.local(self.other, self.final.at[:, self.side(False)]))
        yield


class TableSum:
    def __init__(self, links, table, slots, place, zs, ctxs):
        self.links, self.table, self.slots = links, table, slots
        ctx, z, core = place
        self.hops = (
            [[(ctx, z * 2 + 1 - core)]]
            + [[(ctx, flip(z, o) * 2 + core) for o in range(1, zs)]]
            + [[(flip(ctx, b), z * 2 + core)] for b in bits_of(ctxs)]
        )

    def steps(self):
        slot = 0
        for peers in self.hops:
            flights = []
            for n, peer in enumerate(peers):
                flights.append(
                    self.links.send(self.table, self.slots.at[slot + n], *peer)
                )
            yield
            total = self.table[...]
            for n, flight in enumerate(flights):
                flight.wait_recv()
                flight.wait_send()
                total = total + self.slots[slot + n]
            self.table[...] = total
            slot += len(peers)
        yield


DOWN_SPLIT = 512
BACK_SPLIT = 256
PAIRS = (2, 1, 1, 2)
BACK_PAIRS = (1, 2, 2, None, 1)
PLAN = (
    ("o0", "q0", "u0", "t", "e0", "i1", "o1", "i2", "i3", "tx", "c", "q1", "u1", "o2",),
    ("q2", "cr", "o3", "u2", "q3", "e1",),
    ("d0", "u3", "e2", "qp", "cx", "qf", "op",),
    ("d1", "i4",),
    ("of", "up", "e3",),
    ("uf", "d2", "cy",),
    ("ep", "d3", "P", "ef", "df",),
)
BACK = (
    ("l",),
    (),
    ("l", "d", "e",),
    ("l", "d",),
    ("e",),
    (),
    ("u", "d", "e",),
    (),
    (),
    ("s", "d", "u", "e",),
    (
        "o", "s", "u", "q", "q", "e", "u", "e", "g", "d", "q", "u", "u", "s", "q", "o", "g",
        "e", "o", "l", "g", "o", "q", "q", "s", "g", "e", "q", "o", "o", "u", "s", "u", "g",
        "d", "o", "q", "u", "e", "o", "q", "o", "l", "q", "o", "e", "u",
    ),
)


def layer_kernel(
    ctxs,
    zs,
    pairs,
    back_pairs,
    tok,
    cot,
    order,
    order_block,
    vec_0,
    vec_1,
    vec_2,
    vec_3,
    vec_4,
    vec_5,
    vec_6,
    vec_7,
    vec_8,
    qkv_shard,
    out_shard,
    up_shard,
    down_shard,
    home_out,
    home_grad,
    sum_qkv,
    sum_out,
    sum_up,
    sum_down,
    sum_768,
    sum_wide,
    all_tok,
    all_cot,
    all_out,
    all_grad,
    order_column,
    vectors,
    all_order,
    places,
    route_home,
    route_middle,
    route_cluster,
    rows_out,
    landed,
    all_vectors,
    w_qkv,
    w_out,
    w_up,
    w_down,
    g_down,
    acc,
    inputs,
    low,
    top,
    qkv,
    probs,
    context,
    turned,
    first_norm,
    first_factor,
    hidden,
    slope,
    grad_wide,
    grad_low,
    result_low,
    back_low,
    rows_768,
    row_up,
    small,
    small_slots,
    *rest,
):
    buffers = [rest[5 * n : 5 * n + 5] for n in range(5)]
    send_sem, recv_sem = rest[25:27]
    vec_parts = rest[27:]
    back_split = BACK_SPLIT
    rows, width = tok.shape
    wide = up_shard.shape[1]
    pairs_of_heads = width // LANES
    blocks = rows // CLUSTER
    scale = HEAD_DIM**-0.5
    ctx = lax.axis_index("ctx")
    wsh = lax.axis_index("wsh")
    z, core = wsh // 2, wsh % 2
    place = (ctx, z, core)
    links = Links(send_sem, recv_sem)

    brought = [
        links.local(vector, vec_parts[n])
        for n, vector in enumerate(
            (vec_0, vec_1, vec_2, vec_3, vec_4, vec_5, vec_6, vec_7, vec_8)
        )
    ]
    vectors[...] = jnp.zeros_like(vectors)
    for n, copy in enumerate(brought):
        copy.wait()
        vectors[n : n + 1, 0 : vec_parts[n].shape[0]] = vec_parts[n][...].reshape(1, -1)
    order_column[...] = (
        jnp.broadcast_to(order[...].astype(f32), (LANES, rows)).T.astype(jnp.int32)
    )

    barrier = pltpu.get_barrier_semaphore()
    stream_peers = [
        (ctx, flip(z, o) * 2 + (core if same else 1 - core))
        for o in range(zs)
        for same in (True, False)
        if o > 0 or not same
    ]
    ctx_peers = [(flip(ctx, o), wsh) for o in range(1, ctxs)]
    peers = stream_peers + ctx_peers
    for peer in peers:
        pl.semaphore_signal(barrier, 1, device_id=peer, device_id_type=pl.DeviceIdType.MESH)
    pl.semaphore_wait(barrier, len(peers))

    tok_gather = CtxGather(links, tok, all_tok, ctx, wsh, ctxs, 2)
    cap = route_home.shape[0] // ctxs
    shared = (rows_out, landed, {})
    cot_route, out_route, grad_route = [
        RowRoute(links, buffer, (ctx, wsh), ctxs, cap, shared)
        for buffer in (all_cot, all_out, all_grad)
    ]
    order_flights = [links.send(order_block, all_order.at[ctx], *peer) for peer in ctx_peers]
    vec_own = links.local(vectors, all_vectors.at[wsh])
    vec_flights = [links.send(vectors, all_vectors.at[wsh], *peer) for peer in stream_peers]
    split = DOWN_SPLIT
    parts = [
        (qkv_shard, w_qkv, pairs[0]),
        (out_shard, w_out, pairs[1]),
        (up_shard, w_up, pairs[2]),
        (down_shard.at[:, pl.ds(0, split)], w_down.at[:, pl.ds(0, split)], pairs[3]),
        (
            down_shard.at[:, pl.ds(split, width - split)],
            w_down.at[:, pl.ds(split, width - split)],
            None,
        ),
    ]
    weights = dict(
        zip("quoed", [WeightGather(links, *parts[n], place, zs) for n in (0, 2, 1, 3, 4)])
    )
    rows_in = {"t": tok_gather}

    def act(plan):
        for step in plan:
            if step in routing:
                routing[step]()
                continue
            if step[0] in rows_in:
                gather = rows_in[step[0]]
                if gather.step < gather.steps:
                    gather.advance()
                while step[1:] == "x" and gather.step < gather.steps:
                    gather.advance()
                continue
            gather, kind = weights[step[0]], step[1]
            if kind == "0":
                gather.start()
            elif kind == "3":
                for hop in range(3, zs):
                    gather.hop(hop)
            elif kind in "12":
                gather.hop(int(kind))
            elif kind == "p":
                gather.take_pair()
            else:
                gather.finish()

    def tiles(columns, body, first=0):
        def step(t, carry):
            body(t, pl.ds(pl.multiple_of(t * STEP, STEP), STEP))
            return carry

        lax.fori_loop(first // STEP, columns // STEP, step, 0)

    def token_at(s):
        return lax.broadcasted_iota(jnp.int32, (rows, rows), 0) + s * rows

    def ones_where(condition):
        return jnp.where(condition, 1.0, 0.0).astype(bf16)

    def destinations():
        for flight in order_flights:
            flight.wait_recv()
        all_order[ctx] = order[...]
        places[...] = jnp.zeros_like(places)

        def class_body(d, carry):
            column = jnp.broadcast_to(all_order[d].astype(f32), (LANES, rows)).T
            lane = lax.broadcasted_iota(jnp.int32, (rows, LANES), 1).astype(f32)
            for t in range(ctxs * rows // LANES):
                here = slice(t * LANES, (t + 1) * LANES)
                taken = jnp.where(column == lane + t * LANES, 1.0, 0.0)
                found = jnp.sum(taken, axis=0, keepdims=True)
                places[3:4, here] = places[3:4, here] + found * d.astype(f32)
            return carry

        lax.fori_loop(1, ctxs, class_body, 0)

    def slots():
        def slot_body(once, carry):
            before = route_cluster.at[0:rows]
            before[...] = ones_where(
                lax.broadcasted_iota(jnp.int32, (rows, rows), 0)
                < lax.broadcasted_iota(jnp.int32, (rows, rows), 1)
            )
            row8 = lax.broadcasted_iota(jnp.int32, (8, rows), 0).astype(f32)
            pairs_row = lax.broadcasted_iota(jnp.int32, (ctxs * ctxs, rows), 0).astype(f32)
            gone = jnp.zeros((ctxs * ctxs, 1), f32)
            for s in range(ctxs):
                here = slice(s * rows, (s + 1) * rows)

                def rank(marks):
                    return mm(marks.astype(bf16), before[...])

                to = places[3:4, here]
                mark = jnp.where(row8 == to, 1.0, 0.0)
                turn = jnp.sum(mark * rank(mark), axis=0, keepdims=True) + to + s
                middle = turn - ctxs * jnp.floor(turn * (1.0 / ctxs))
                mark = jnp.where(row8 == middle, 1.0, 0.0)
                places[0:1, here] = middle
                places[1:2, here] = jnp.sum(mark * rank(mark), axis=0, keepdims=True)
                mark = jnp.where(pairs_row == middle * ctxs + to, 1.0, 0.0)
                places[2:3, here] = jnp.sum(mark * (rank(mark) + gone), axis=0, keepdims=True)
                gone = gone + jnp.sum(mark, axis=1, keepdims=True)
            mine = pl.ds(pl.multiple_of(ctx * rows, LANES), rows)
            code = (places[0:1, mine] * cap + places[1:2, mine]).astype(jnp.int32)
            route_home[...] = ones_where(slot_row(ctxs) == code)
            return carry

        lax.fori_loop(0, 1, slot_body, 0)

    def slot_row(blocks_of):
        return lax.broadcasted_iota(jnp.int32, (blocks_of * cap, rows), 0)

    def middle_route():
        def middle_body(s, carry):
            here = pl.ds(pl.multiple_of(s * rows, LANES), rows)
            middle, first, second, to = [
                places[n : n + 1, here].astype(jnp.int32) for n in range(4)
            ]
            coming = ones_where((slot_row(1) == first) & (middle == ctx))
            going = ones_where(slot_row(ctxs) == to * cap + second)
            at = pl.ds(pl.multiple_of(s * cap, 16), cap)
            route_middle[at, :] = mm_nt(coming, going).astype(bf16)
            return carry

        lax.fori_loop(0, ctxs, middle_body, 0)

    def cluster_route():
        route_cluster[...] = jnp.zeros_like(route_cluster)

        def cluster_body(s, carry):
            here = pl.ds(pl.multiple_of(s * rows, LANES), rows)
            code = (places[0:1, here] * cap + places[2:3, here]).astype(jnp.int32)
            sits = ones_where(slot_row(ctxs) == code)
            taken = ones_where(order[...] == token_at(s))
            route_cluster[...] = (route_cluster[...].astype(f32) + mm(sits, taken)).astype(bf16)
            return carry

        lax.fori_loop(0, ctxs, cluster_body, 0)

    def hop(route, phase, product, matrix, source):
        route.free(phase)

        def sort_rows(t, span):
            rows_out[phase, :, span] = product(matrix[...], source[:, span]).astype(bf16)

        tiles(width, sort_rows)
        route.send(phase)

    def arrive(route, product, matrix, target):
        route.collect(1)

        def place_rows(t, span):
            target[:, span] = product(matrix[...], landed[:, span]).astype(bf16)

        tiles(width, place_rows)

    def cot_first():
        links.local(cot, landed.at[0:rows]).wait()
        hop(cot_route, 0, mm, route_home, landed.at[0:rows])

    def cot_second():
        cot_route.collect(0)
        hop(cot_route, 1, mm_tn, route_middle, landed)

    def cot_last():
        arrive(cot_route, mm_tn, route_cluster, top)

    routing = {
        "i1": destinations,
        "i2": slots,
        "i3": middle_route,
        "i4": cluster_route,
        "c": cot_first,
        "cr": functools.partial(cot_route.forward, 0),
        "cx": cot_second,
        "cy": functools.partial(cot_route.forward, 1),
        "P": cot_last,
    }

    leaving = []

    def go_home(route, source, buffer, target):
        hop(route, 0, mm, route_cluster, source)
        yield
        route.forward(0)
        yield
        route.collect(0)
        hop(route, 1, mm, route_middle, landed)
        yield
        route.forward(1)
        yield
        arrive(route, mm_tn, route_home, buffer)
        leaving.append(links.local(buffer, target))
        yield

    act(PLAN[0])
    vec_own.wait()
    for flight in vec_flights:
        flight.wait_recv()

    rows_768[...] = jnp.zeros_like(rows_768)
    row_up[...] = jnp.zeros_like(row_up)
    length = width // (2 * zs)

    def spread(part, spot, size, target):
        first = min(spot // LANES * LANES, target.shape[1] - 2 * part.shape[1])
        shape = (part.shape[1], 2 * part.shape[1])
        j = lax.broadcasted_iota(jnp.int32, shape, 0)
        col = lax.broadcasted_iota(jnp.int32, shape, 1)
        move = jnp.where((col == j + (spot - first)) & (j < size), 1.0, 0.0).astype(bf16)
        at = pl.ds(first, shape[1])
        target[:, at] = target[:, at] + mm(part, move)[: target.shape[0]]

    length_up = wide // (2 * zs)
    for s in range(2 * zs):
        spread(all_vectors[s, :, 0:LANES], length * s, length, rows_768)
        if length_up % LANES == 0:
            up_part = all_vectors[s, 8:16, 0:length_up].astype(f32)
            row_up[0:1, length_up * s : length_up * (s + 1)] = up_part[0:1]
        else:
            spread(all_vectors[s, 8:16, :], length_up * s, length_up, row_up)

    def pick(gather, own, total):
        copies = {}
        stage = (result_low, back_low)

        def fetch(offset):
            if offset == 0:
                src = own
            else:
                gather.need(offset)
                src = gather.buffer.at[flip(ctx, offset)]
            copies[offset] = links.local(src, stage[offset % 2])

        fetch(0)
        for offset in range(ctxs):
            copies[offset].wait()
            if offset + 1 < ctxs:
                fetch(offset + 1)
            first = flip(ctx, offset) * rows

            def body(i, carry):
                here = pl.ds(pl.multiple_of(i * CLUSTER, CLUSTER), CLUSTER)
                place_of = order_column[here, :]
                lane = lax.broadcasted_iota(jnp.int32, (CLUSTER, LANES), 1)
                chosen = jnp.concatenate(
                    [
                        jnp.where(place_of == lane + (first + t * LANES), 1.0, 0.0).astype(bf16)
                        for t in range(rows // LANES)
                    ],
                    axis=1,
                )
                got = mm(chosen, stage[offset % 2][...])
                total[here, :] = got if offset == 0 else total[here, :] + got
                return carry

            lax.fori_loop(0, blocks, body, 0)

    def row_pass(size, body):
        def step(i, carry):
            body(pl.ds(pl.multiple_of(i * size, size), size))
            return carry

        lax.fori_loop(0, rows // size, step, 0)

    def tally(vector, values):
        total = jnp.sum(values, axis=0, keepdims=True)
        for t in range(width // STEP):
            at = pl.ds(vector * (width // STEP) + t, 1)
            small[at, :] = small[at, :] + total[:, t * STEP : (t + 1) * STEP]

    small[...] = jnp.zeros_like(small)
    qbias, vbias, obias, gain1, shift1, dbias, gain2, shift2 = [
        rows_768.at[pl.ds(n, 1)] for n in range(8)
    ]

    act(PLAN[1])
    pick(tok_gather, tok, acc)

    def keep_inputs(here):
        inputs[here, :] = acc[here, :].astype(bf16)

    row_pass(CLUSTER, keep_inputs)
    act(PLAN[2])

    def project(t, span):
        at = pl.ds(pl.multiple_of((t % (width // STEP)) * STEP, STEP), STEP)
        part = t // (width // STEP)
        bias = jnp.where(part == 0, qbias[:, at], jnp.where(part == 2, vbias[:, at], 0.0))
        qkv[:, span] = (mm(inputs[...], w_qkv[:, span]) + bias).astype(bf16)

    tiles(3 * width, project)

    act(PLAN[3])

    lane = lax.broadcasted_iota(jnp.int32, (1, LANES), 1)
    left = jnp.where(lane < HEAD_DIM, 1.0, 0.0).astype(bf16)
    right = jnp.where(lane < HEAD_DIM, 0.0, 1.0).astype(bf16)

    def both(values):
        return jnp.concatenate([values * left, values * right], axis=0)

    def side_by_side(values):
        return jnp.concatenate([values[:CLUSTER], values[CLUSTER:]], axis=1)

    def part_of(here, kind, pair):
        return qkv[here, kind * width + pair * LANES : kind * width + (pair + 1) * LANES]

    def attend(b, carry):
        here = pl.ds(pl.multiple_of(b * CLUSTER, CLUSTER), CLUSTER)
        visible = order[0:1, here] <= order_column[here, :]
        hide = jnp.where(visible, 0.0, -1e30)
        hide = jnp.concatenate([hide, hide], axis=0)
        for pair in range(pairs_of_heads):
            query, keyed, valued = [part_of(here, kind, pair) for kind in range(3)]
            scores = mm_nt(both(query), keyed) * scale + hide
            expd = jnp.exp(scores - jnp.max(scores, axis=1, keepdims=True))
            prob = expd * (1.0 / jnp.sum(expd, axis=1, keepdims=True))
            probs[b * pairs_of_heads + pair] = prob
            got = mm(side_by_side(prob.astype(bf16)), both(valued))
            context[here, pair * LANES : (pair + 1) * LANES] = got.astype(bf16)
        return carry

    lax.fori_loop(0, blocks, attend, 0)
    act(PLAN[4])

    def out_project(t, span):
        acc[:, span] = mm(context[...], w_out[:, span])

    tiles(width, out_project)

    def first_normalize(here):
        attended = (acc[here, :] + obias[...]).astype(bf16).astype(f32)
        resid = inputs[here, :].astype(f32) + attended
        centre = resid - jnp.mean(resid, axis=1, keepdims=True)
        factor = lax.rsqrt(jnp.mean(centre * centre, axis=1, keepdims=True) + epsilon)
        normed = centre * factor
        first_norm[here, :] = normed
        first_factor[here, :] = factor
        low[here, :] = (normed * gain1[...] + shift1[...]).astype(bf16)

    row_pass(64, first_normalize)
    act(PLAN[5])

    def feed(t, span):
        pre = mm(low[...], w_up[:, span]) + row_up[0:1, span]
        half = 0.5 * (1.0 + lax.erf(pre * 0.7071067811865476))
        hidden[:, span] = (pre * half).astype(bf16)
        slope[:, span] = (half + pre * jnp.exp(-0.5 * pre * pre) * 0.3989422804014327).astype(bf16)

    tiles(wide, feed)
    act(PLAN[6])

    def down(t, span):
        acc[:, span] = mm(hidden[...], w_down[:, span])

    tiles(width, down)

    def second_normalize(here):
        first_out = first_norm[here, :] * gain1[...] + shift1[...]
        second_in = first_out + acc[here, :] + dbias[...]
        centre = second_in - jnp.mean(second_in, axis=1, keepdims=True)
        factor = lax.rsqrt(jnp.mean(centre * centre, axis=1, keepdims=True) + epsilon)
        normed = centre * factor
        result_low[here, :] = (normed * gain2[...] + shift2[...]).astype(bf16)
        grad_top = top[here, :].astype(f32)
        tally(6, grad_top * normed)
        tally(7, grad_top)
        grad_normed = grad_top * gain2[...]
        grad = factor * (
            grad_normed
            - jnp.mean(grad_normed, axis=1, keepdims=True)
            - normed * jnp.mean(grad_normed * normed, axis=1, keepdims=True)
        )
        grad_wide[here, :] = grad
        grad = grad.astype(bf16)
        grad_low[here, :] = grad
        tally(5, grad.astype(f32))

    row_pass(64, second_normalize)

    scatters = [
        GradScatter(links, w, f, b, place, zs, ctxs, p)
        for w, f, b, p in zip(
            (
                w_qkv,
                w_out,
                w_up,
                g_down.at[:, pl.ds(0, back_split)],
                g_down.at[:, pl.ds(back_split, width - back_split)],
            ),
            (
                sum_qkv,
                sum_out,
                sum_up,
                sum_down.at[:, pl.ds(0, back_split)],
                sum_down.at[:, pl.ds(back_split, width - back_split)],
            ),
            buffers,
            back_pairs,
        )
    ]
    gathered, links.sent = links.sent, []
    back = {}

    def go(plan):
        for step in plan:
            if step in back:
                next(back[step], None)

    back["l"] = go_home(out_route, result_low, low, home_out)
    go(BACK[0])
    part_rows = wide // (2 * zs)

    def down_grad(owner):
        def body(i, carry):
            here = pl.ds(pl.multiple_of((i * 2 + owner) * part_rows, LANES // 2), part_rows)
            turned_hidden = hidden_turned(i * 2 + owner)
            g_down[here, :] = mm(turned_hidden, grad_low[...]).astype(bf16)
            return carry

        lax.fori_loop(0, zs, body, 0)

    if part_rows % LANES == 0:

        def hidden_turned(s):
            return hidden[:, pl.ds(pl.multiple_of(s * part_rows, LANES), part_rows)].T

        down_grad(1 - core)
        scatters[3].send_core()
        scatters[4].send_core()
        down_grad(core)
    else:

        def all_down(t, span):
            g_down[span, :] = mm(hidden[:, span].T, grad_low[...]).astype(bf16)

        tiles(wide, all_down)
        scatters[3].send_core()
        scatters[4].send_core()

    def back_hidden(t, span):
        grad = (mm_nt(grad_low[...], w_down[span, :]) * slope[:, span]).astype(bf16)
        slope[:, span] = grad
        small[pl.ds(8 * (width // STEP) + t, 1), :] = jnp.sum(
            grad.astype(f32), axis=0, keepdims=True
        )

    tiles(wide // 2, back_hidden)
    back["d"] = scatters[3].steps()
    back["e"] = scatters[4].steps()
    go(BACK[1])
    tiles(wide, back_hidden, wide // 2)
    go(BACK[2])

    def back_up(t, span):
        acc[:, span] = mm_nt(slope[...], w_up[span, :])

    tiles(width, back_up)

    def first_back(here):
        grad_first = grad_wide[here, :] + acc[here, :]
        normed = first_norm[here, :]
        tally(3, grad_first * normed)
        tally(4, grad_first)
        grad_normed = grad_first * gain1[...]
        grad = first_factor[here, :] * (
            grad_normed
            - jnp.mean(grad_normed, axis=1, keepdims=True)
            - normed * jnp.mean(grad_normed * normed, axis=1, keepdims=True)
        )
        grad_wide[here, :] = grad
        grad = grad.astype(bf16)
        grad_low[here, :] = grad
        tally(2, grad.astype(f32))

    row_pass(64, first_back)
    go(BACK[3])
    for flight in gathered:
        flight.wait_send()

    turned[...] = low[...].T

    def up_grad(t, span):
        w_up[:, span] = mm(turned[...], slope[:, span]).astype(bf16)

    tiles(wide, up_grad)
    scatters[2].send_core()
    back["u"] = scatters[2].steps()

    turned[...] = context[...].T

    def back_context(t, span):
        context[:, span] = mm_nt(grad_low[...], w_out[span, :]).astype(bf16)

    tiles(width, back_context)

    def out_grad(t, span):
        w_out[:, span] = mm(turned[...], grad_low[:, span]).astype(bf16)

    tiles(width, out_grad)
    scatters[1].send_core()
    back["o"] = scatters[1].steps()
    go(BACK[4])

    def back_attend(b, carry):
        here = pl.ds(pl.multiple_of(b * CLUSTER, CLUSTER), CLUSTER)
        for pair in range(pairs_of_heads):
            query, keyed, valued = [part_of(here, kind, pair) for kind in range(3)]
            prob = probs[b * pairs_of_heads + pair]
            grad = both(context[here, pair * LANES : (pair + 1) * LANES])
            grad_prob = mm_nt(grad, valued)
            grad_valued = mm_tn(prob.astype(bf16), grad)
            inner = jnp.sum(prob * grad_prob, axis=1, keepdims=True)
            grad_score = (prob * (grad_prob - inner)).astype(bf16)
            grad_query = mm(side_by_side(grad_score), both(keyed)) * scale
            grad_keyed = mm_tn(grad_score, both(query)) * scale
            for kind, value in enumerate((grad_query, grad_keyed, grad_valued)):
                at = kind * width + pair * LANES
                qkv[here, at : at + LANES] = value.astype(bf16)
        return carry

    for b in range(blocks):
        lax.fori_loop(b, b + 1, back_attend, 0)
        go(BACK[5 + min(b, 3)])

    def input_sums(here):
        tally(0, qkv[here, 0:width].astype(f32))
        tally(1, qkv[here, 2 * width : 3 * width].astype(f32))

    row_pass(64, input_sums)

    def back_qkv(t, span):
        back_low[:, span] = (mm_nt(qkv[...], w_qkv[span, :]) + grad_wide[:, span]).astype(bf16)

    table = TableSum(links, small, small_slots, place, zs, ctxs)
    back["s"] = table.steps()
    tiles(width, back_qkv)
    go(BACK[9])
    turned[...] = inputs[...].T

    def qkv_grad(t, span):
        w_qkv[:, span] = mm(turned[...], qkv[:, span]).astype(bf16)

    tiles(3 * width, qkv_grad)
    scatters[0].send_core()
    back["q"] = scatters[0].steps()
    back["g"] = go_home(grad_route, back_low, top, home_grad)
    go(BACK[10])
    running = list(back.values())
    while running:
        running = [steps for steps in running if next(steps, "end") != "end"]
    count = width // STEP
    for n in range(8):
        for t in range(count):
            sum_768[n : n + 1, t * STEP : (t + 1) * STEP] = small[n * count + t : n * count + t + 1]
    for t in range(wide // STEP):
        sum_wide[0:1, t * STEP : (t + 1) * STEP] = small[8 * count + t : 8 * count + t + 1]
    links.drain()
    for copy in leaving:
        copy.wait()
    for scatter in scatters:
        for result in scatter.results:
            result.wait()


def finish_kernel(wshs, *refs):
    sources, (sum_768, sum_wide) = refs[:6], refs[6:8]
    targets, vecs = refs[8:14], refs[14:23]
    taken, given, sem = refs[23:29], refs[29:35], refs[35]
    coming = [pltpu.make_async_copy(s, t, sem.at[n]) for n, (s, t) in enumerate(zip(sources, taken))]
    for copy in coming:
        copy.start()
    me = lax.axis_index("wsh")
    for sums, outs in ((sum_768, vecs[:8]), (sum_wide, vecs[8:])):
        size = outs[0].shape[0]
        columns = sums.shape[1]
        mine = pltpu.roll(sums[...], lax.rem(columns - me * size, columns), 1)
        for n, out in enumerate(outs):
            out[...] = mine[n, 0:size]
    going = []
    for n, copy in enumerate(coming):
        copy.wait()
        given[n][...] = taken[n][...].astype(given[n].dtype)
        going.append(pltpu.make_async_copy(given[n], targets[n], sem.at[6 + n]))
        going[-1].start()
    for copy in going:
        copy.wait()


def on_device(
    ctxs,
    wshs,
    tokens,
    cluster_order,
    qkv_weight,
    query_bias,
    value_bias,
    out_weight,
    out_bias,
    first_gain,
    first_shift,
    up_weight,
    up_bias,
    down_weight,
    down_bias,
    second_gain,
    second_shift,
    cotangent,
):
    rows, width = tokens.shape[1:]
    wide = up_weight.shape[1]
    zs = wshs // 2
    small_rows = 8 * (width // STEP) + wide // STEP
    small_rows = (small_rows + 7) // 8 * 8
    vector_lanes = (up_bias.shape[0] + LANES - 1) // LANES * LANES
    heads_pairs = width // LANES
    blocks = rows // CLUSTER
    hops = zs + len(bits_of(ctxs))
    shards = [qkv_weight.shape, out_weight.shape, up_weight.shape, down_weight.shape]
    sems = 2 * wshs + 4 * 2 * ctxs * 2 + 10 * zs * 4 + 4 * (4 * zs + 8) + 64

    def vmem(shape, dtype=bf16):
        return pltpu.VMEM(shape, dtype)

    pairs, back_pairs = PAIRS, BACK_PAIRS
    landing = []
    rows_down = down_weight.shape[0]
    pieces = shards[:3] + [(rows_down, BACK_SPLIT), (rows_down, width - BACK_SPLIT)]
    for (n, columns), pair in zip(pieces, back_pairs):
        part = columns // 2
        landing.append(vmem((zs, n, columns)))
        if pair is None:
            landing.append(vmem((1, 16, LANES)))
            landing.append(vmem((zs - 1, n, columns)))
            landing.append(vmem((len(bits_of(ctxs)), n, columns)))
            landing.append(vmem((16, LANES)))
        else:
            landing.append(vmem((zs, n, part)))
            landing.append(vmem((zs - 1, n, part)))
            landing.append(vmem((len(bits_of(ctxs)) - 1, n, part)))
            landing.append(vmem((n, part)))
    anywhere = pl.BlockSpec(memory_space=pl.ANY)
    on_chip = pl.BlockSpec(memory_space=pltpu.VMEM)
    many = jax.ShapeDtypeStruct((ctxs, rows, width), bf16)
    cap = (rows // ctxs + ctxs - 1 + 15) // 16 * 16
    routed = jax.ShapeDtypeStruct((2 * ctxs + 2, cap, width), bf16)
    results = pl.pallas_call(
        functools.partial(layer_kernel, ctxs, zs, pairs, back_pairs),
        out_shape=[
            jax.ShapeDtypeStruct((rows, width), bf16),
            jax.ShapeDtypeStruct((rows, width), bf16),
        ]
        + [jax.ShapeDtypeStruct(s, bf16) for s in shards]
        + [jax.ShapeDtypeStruct((8, width), f32), jax.ShapeDtypeStruct((8, wide), f32)]
        + [many] + [routed] * 3,
        in_specs=[anywhere, anywhere, on_chip, anywhere] + [anywhere] * 13,
        out_specs=[anywhere] * 6 + [on_chip] * 2 + [anywhere] * 4,
        scratch_shapes=[
            vmem((rows, LANES), jnp.int32),
            vmem((16, vector_lanes)),
            vmem((ctxs, 1, rows), jnp.int32),
            vmem((8, ctxs * rows), f32),
            vmem((ctxs * cap, rows)),
            vmem((ctxs * cap, ctxs * cap)),
            vmem((ctxs * cap, rows)),
            vmem((2, ctxs * cap, width)),
            vmem((ctxs * cap, width)),
            vmem((wshs, 16, vector_lanes)),
            vmem((width, 3 * width)),
            vmem((width, width)),
            vmem((width, wide)),
            vmem((wide, width)),
            vmem((wide, width)),
            vmem((rows, width), f32),
            vmem((rows, width)),
            vmem((rows, width)),
            vmem((rows, width)),
            vmem((rows, 3 * width)),
            vmem((blocks * heads_pairs, 2 * CLUSTER, CLUSTER), f32),
            vmem((rows, width)),
            vmem((width, rows)),
            vmem((rows, width), f32),
            vmem((rows, 1), f32),
            vmem((rows, wide)),
            vmem((rows, wide)),
            vmem((rows, width), f32),
            vmem((rows, width)),
            vmem((rows, width)),
            vmem((rows, width)),
            vmem((8, width), f32),
            vmem((8, wide), f32),
            vmem((small_rows, STEP), f32),
            vmem((hops, small_rows, STEP), f32),
        ]
        + landing
        + [pltpu.SemaphoreType.DMA((sems,)), pltpu.SemaphoreType.DMA((sems,))]
        + [vmem(query_bias.shape)] * 8
        + [vmem(up_bias.shape)],
        compiler_params=pltpu.CompilerParams(
            collective_id=0, has_side_effects=True, vmem_limit_bytes=67043328
        ),
        name="layer",
    )(
        tokens[0],
        cotangent[0],
        cluster_order,
        cluster_order,
        query_bias,
        value_bias,
        out_bias,
        first_gain,
        first_shift,
        down_bias,
        second_gain,
        second_shift,
        up_bias,
        qkv_weight,
        out_weight,
        up_weight,
        down_weight,
    )
    big = results[:6]
    part = width // wshs
    part_wide = wide // wshs
    outs = [jax.ShapeDtypeStruct((rows, width), bf16), jax.ShapeDtypeStruct((rows, width), f32)]
    outs += [jax.ShapeDtypeStruct(s, f32) for s in shards]
    outs += [jax.ShapeDtypeStruct((part,), f32)] * 8 + [jax.ShapeDtypeStruct((part_wide,), f32)]
    (home_out, home_grad, g_qkv, g_out, g_up, g_down, *vecs) = pl.pallas_call(
        functools.partial(finish_kernel, wshs),
        out_shape=outs,
        in_specs=[anywhere] * 6 + [on_chip] * 2,
        out_specs=[anywhere] * 6 + [on_chip] * 9,
        scratch_shapes=[vmem(v.shape) for v in big]
        + [vmem(v.shape, o.dtype) for v, o in zip(big, outs)]
        + [pltpu.SemaphoreType.DMA((12,))],
        compiler_params=pltpu.CompilerParams(vmem_limit_bytes=67043328),
        name="finish",
    )(*big, *results[6:8])
    g_q, g_v, g_o, g_g1, g_s1, g_d, g_g2, g_s2, g_u = vecs
    return (
        home_out[None],
        home_grad[None],
        g_qkv,
        g_q,
        g_v,
        g_out,
        g_o,
        g_g1,
        g_s1,
        g_up,
        g_u,
        g_down,
        g_d,
        g_g2,
        g_s2,
    )


def solution(mesh):
    row = P("wsh", None)
    vec = P("wsh")
    seq = P("wsh", "ctx", None)
    in_specs = (
        seq,
        P("wsh", "ctx"),
        row,
        vec,
        vec,
        row,
        vec,
        vec,
        vec,
        row,
        vec,
        row,
        vec,
        vec,
        vec,
        seq,
    )
    out_specs = (
        seq,
        seq,
        row,
        vec,
        vec,
        row,
        vec,
        vec,
        vec,
        row,
        vec,
        row,
        vec,
        vec,
        vec,
    )
    return jax.shard_map(
        functools.partial(on_device, mesh.shape["ctx"], mesh.shape["wsh"]),
        mesh=mesh,
        in_specs=in_specs,
        out_specs=out_specs,
        check_vma=False,
    )
```
